256 devices in a mesh: ctx: 32 (over y, x, core), tp: 8 (over z).
Axes of the slice: x: 4, y: 4, z: 8, core: 2. Of those that a mesh axis runs over, the one named last changes fastest.
Arguments:
- hidden: bfloat16 [16384, 8192], P('ctx', 'tp'), may hold values from -6 to 6
- queries: bfloat16 [16384, 8192], P('ctx', 'tp'), may hold values from -6.5 to 6.5
- rotated_keys: bfloat16 [16384, 1024], P('ctx', 'tp'), may hold values from -6 to 6
- frozen_value_rows: bfloat16 [16384, 1024], P('ctx', 'tp'), may hold values from -6 to 6
- adapter_a_v: bfloat16 [8192, 16], P('tp'), may hold values from -0.0625 to 0.0625
- value_up_matrix: bfloat16 [16, 1024], P(None, 'tp'), may hold values from -1.5 to 1.5
- adapter_a_o: bfloat16 [8192, 16], P('tp'), may hold values from -0.0625 to 0.0625
- output_up_matrix: bfloat16 [16, 8192], P(None, 'tp'), may hold values from -1.5 to 1.5
- doc_lengths: int32 [64], replicated, may hold values from 1 to 1536, 16384 in all
- pair_slots: int32 [64], replicated, may hold values from 0 to 63, each once
- token_logratio: float32 [16384], P('ctx'), may hold values from -0.6 to 0.6
- out_cotangent: bfloat16 [16384, 8192], P('ctx', 'tp'), may hold values from -6 to 6
- attn_cotangent: bfloat16 [16384, 8192], P('ctx', 'tp'), may hold values from -6 to 6
Outputs:
- attention_output_rows: bfloat16 [16384, 8192], P('ctx', 'tp')
- output_adapter_term: bfloat16 [16384, 8192], P('ctx', 'tp')
- input_adapter_gradient: bfloat16 [16384, 8192], P('ctx', 'tp')
- value_down_gradient: float32 [8192, 16], P('tp')
- value_up_gradient: float32 [16, 1024], P(None, 'tp')
- output_down_gradient: float32 [8192, 16], P('tp')
- output_up_gradient: float32 [16, 8192], P(None, 'tp')
The draws below stay inside these ranges and needn't reach their ends.
Inputs may be any that keep to these rules, and one draw needn't show every extreme that they name: `doc_lengths`: the lengths sum to 16384, and the longest document has exactly 1536 tokens. `pair_slots`: each value once; the documents with slots 2p and 2p + 1 answer the same prompt, the even slot being the chosen answer and the odd one the rejected answer.
All inputs are finite; a program needn't handle non-finite values.
Results may differ from the reference program's by a relative error of at most 0.022.
Values may be sent and summed in bfloat16 or wider, within the bound.
No kernel may reach another device: no remote copies, remote signals or barrier semaphores. Data moves between devices by JAX's collectives and lax.ppermute only.
A program may use at most 128 MiB of HBM per device.

```python
import math
import jax
import jax.numpy as jnp
import numpy as np
from jax import lax

D = 8192
HEADS = 64
KV_HEADS = 8
HD = 128
RANK = 16
TOK_DEV = 512
TOKENS = 16384
MAXDOC = 1536
NDOCS = 64
N_CTX = 32


def draw_rotated_keys(key, part):
    fresh = jax.random.fold_in(key, 11)
    result = jnp.clip(jax.random.normal(fresh, (TOKENS, KV_HEADS * HD), jnp.float32), -6.0, 6.0)
    return result.astype(jnp.bfloat16)


def draw_queries(key, part):
    fresh = jax.random.fold_in(key, 13)
    result = jnp.clip(jax.random.normal(fresh, (TOKENS, HEADS * HD), jnp.float32), -6.0, 6.0)
    return result.astype(jnp.bfloat16)


def steps_of(own_key, extent, split, low, high):
    gain, own = 1.0, jax.random.fold_in(own_key, 6)
    for dim, blocks in split:
        draws = jnp.exp(jax.random.uniform(jax.random.fold_in(own, dim), (blocks,), jnp.float32, low / len(split), high / len(split)))
        gain = gain * jnp.repeat(draws, extent[dim] // blocks).reshape([-1 if axis == dim else 1 for axis in range(len(extent))])
    return gain


def split_up(count, total, most, lean):
    loads = [(1 << 20) // math.isqrt(grade ** lean) + 1 for grade in range(2, count + 1)]
    surplus, counts = total - most - (count - 1), [1] * (count - 1)
    while surplus > 0:
        movable = [i for i in range(count - 1) if counts[i] < most]
        whole, left = sum([loads[i] for i in movable]), surplus
        for i in movable:
            addition = min(most - counts[i], max(1, left * loads[i] // whole), surplus)
            counts[i] = counts[i] + addition
            surplus = surplus - addition
    return np.array([most] + counts)


def uneven(stream_key, number_of, total, bound, lean):
    if number_of == 2:
        one = jax.random.randint(stream_key, (), max(1, total - bound), min(bound, total - 1) + 1)
        return jnp.stack([one, total - one])
    sizes = jnp.asarray(split_up(number_of, total, bound, lean), jnp.int32)
    pairs = (number_of - 1) // 2
    donor, receiver = sizes[1:1 + 2 * pairs:2], sizes[2:2 + 2 * pairs:2]
    room = jnp.minimum(donor - 1, bound - receiver)
    passed = jax.random.randint(jax.random.fold_in(stream_key, 1), (pairs,), 0, 1 << 20) % (room + 1)
    sizes = sizes.at[1:1 + 2 * pairs:2].set(donor - passed).at[2:2 + 2 * pairs:2].set(receiver + passed)
    return sizes[jax.random.permutation(jax.random.fold_in(stream_key, 2), number_of)]


def gaussian(own_key, extent, width, most, cuts=(), held_as=jnp.bfloat16):
    entries = width * jax.random.normal(own_key, extent, jnp.float32)
    if cuts:
        entries = entries * steps_of(own_key, extent, cuts, -0.22, 0.18)
    return jnp.clip(entries, -most, most).astype(held_as)


def setup_inputs(seed: int = 0) -> dict:
    splits = jax.random.split(jax.random.key(seed), 14)
    hidden = gaussian(splits[0], (TOKENS, D), 1.0, 6.0, ((0, 32), (1, 8)))
    queries = draw_queries(jax.random.fold_in(splits[13], 71), 0)
    rotated_keys = draw_rotated_keys(jax.random.fold_in(splits[13], 71), 0)
    frozen_value_rows = gaussian(splits[3], (TOKENS, KV_HEADS * HD), 1.0, 6.0, ((0, 32), (1, 8)))
    adapter_a_v = gaussian(splits[4], (D, RANK), D ** -0.5, 0.0625, ((0, 8),))
    value_up_matrix = gaussian(splits[5], (RANK, KV_HEADS * HD), RANK ** -0.5, 1.5, ((1, 8),))
    adapter_a_o = gaussian(splits[6], (HEADS * HD, RANK), (HEADS * HD) ** -0.5, 0.0625, ((0, 8),))
    output_up_matrix = gaussian(splits[7], (RANK, D), RANK ** -0.5, 1.5, ((1, 8),))
    doc_lengths = uneven(splits[8], NDOCS, TOKENS, MAXDOC, 2).astype(jnp.int32)
    pair_slots = jax.random.permutation(splits[9], NDOCS).astype(jnp.int32)
    token_logratio = gaussian(splits[10], (TOKENS,), 0.1, 0.6, ((0, 32),), jnp.float32)
    out_cotangent = gaussian(splits[11], (TOKENS, D), 1.0, 6.0, ((0, 32), (1, 8)))
    attn_cotangent = gaussian(splits[12], (TOKENS, HEADS * HD), 1.0, 6.0, ((0, 32), (1, 8)))
    return dict(hidden=hidden, queries=queries, rotated_keys=rotated_keys, frozen_value_rows=frozen_value_rows, adapter_a_v=adapter_a_v, value_up_matrix=value_up_matrix, adapter_a_o=adapter_a_o, output_up_matrix=output_up_matrix, doc_lengths=doc_lengths, pair_slots=pair_slots, token_logratio=token_logratio, out_cotangent=out_cotangent, attn_cotangent=attn_cotangent)


ADAPTER_SCALE = 2.0
BETA = 0.5
NEG_FILL = -1e+30

def doc_index(positions, doc_ends):
    return lax.optimization_barrier(jnp.sum((doc_ends[None, :] <= positions[:, None]).astype(jnp.int32), axis=1))

def doc_weights(margins, pair_slots):
    pair_ids = pair_slots // 2
    signs = jnp.where(pair_slots % 2 == 0, 1.0, -1.0).astype(jnp.float32)
    same_pair = (pair_ids[:, None] == pair_ids[None, :]).astype(jnp.float32)
    gaps = lax.optimization_barrier(jnp.sum(same_pair * (signs * margins)[None, :], axis=1))
    return -BETA * signs * jax.nn.sigmoid(-BETA * gaps)

def reference(hidden, queries, rotated_keys, frozen_value_rows, adapter_a_v, value_up_matrix, adapter_a_o, output_up_matrix, doc_lengths, pair_slots, token_logratio, out_cotangent, attn_cotangent):
    group_size = HEADS // KV_HEADS
    front_pad = 3 * TOK_DEV
    kv_width = KV_HEADS * HD
    score_scale = 1.0 / math.sqrt(HD)
    doc_ends = jnp.cumsum(doc_lengths).astype(jnp.int32)
    positions = jnp.arange(TOKENS, dtype=jnp.int32)
    doc_ids = doc_index(positions, doc_ends)
    onehot = (doc_ids[:, None] == jnp.arange(NDOCS, dtype=jnp.int32)[None, :]).astype(jnp.float32)
    margins = lax.optimization_barrier(jnp.sum(onehot * token_logratio[:, None], axis=0))
    token_weight = lax.optimization_barrier(jnp.sum(onehot * doc_weights(margins, pair_slots)[None, :], axis=1))
    value_down_rows = jnp.dot(hidden, adapter_a_v, preferred_element_type=jnp.float32).astype(jnp.bfloat16)
    value_rows = (frozen_value_rows.astype(jnp.float32) + ADAPTER_SCALE * jnp.dot(value_down_rows, value_up_matrix, preferred_element_type=jnp.float32)).astype(jnp.bfloat16)
    output_gradient_rows = (token_weight[:, None] * out_cotangent.astype(jnp.float32)).astype(jnp.bfloat16)
    output_down_row_gradient = (ADAPTER_SCALE * jnp.dot(output_gradient_rows, output_up_matrix.T, preferred_element_type=jnp.float32)).astype(jnp.bfloat16)
    attn_grad = (token_weight[:, None] * attn_cotangent.astype(jnp.float32) + jnp.dot(output_down_row_gradient, adapter_a_o.T, preferred_element_type=jnp.float32)).astype(jnp.bfloat16)
    padded_keys = jnp.concatenate([jnp.zeros((front_pad, kv_width), jnp.bfloat16), rotated_keys], axis=0)
    padded_values = jnp.concatenate([jnp.zeros((front_pad, kv_width), jnp.bfloat16), value_rows], axis=0)

    def block_step(carried, block_index):
        first_row = (block_index * TOK_DEV).astype(jnp.int32)
        query_pos = first_row + jnp.arange(TOK_DEV, dtype=jnp.int32)
        key_pos = first_row - front_pad + jnp.arange(4 * TOK_DEV, dtype=jnp.int32)
        query_doc = doc_index(query_pos, doc_ends)
        key_doc = doc_index(key_pos, doc_ends)
        allowed = (query_doc[:, None] == key_doc[None, :]) & (key_pos[None, :] <= query_pos[:, None]) & (key_pos[None, :] >= 0)
        query_block = lax.dynamic_slice_in_dim(queries, first_row, TOK_DEV, 0).astype(jnp.float32).reshape(TOK_DEV, KV_HEADS, group_size, HD)
        key_block = lax.dynamic_slice_in_dim(padded_keys, first_row, 4 * TOK_DEV, 0).astype(jnp.float32).reshape(4 * TOK_DEV, KV_HEADS, HD)
        value_block = lax.dynamic_slice_in_dim(padded_values, first_row, 4 * TOK_DEV, 0).astype(jnp.float32).reshape(4 * TOK_DEV, KV_HEADS, HD)
        scores = jnp.einsum('ikgd,jkd->kgij', query_block, key_block) * score_scale
        scores = jnp.where(allowed[None, None], scores, NEG_FILL)
        row_top = lax.optimization_barrier(jnp.max(scores, axis=-1, keepdims=True))
        exponent = jnp.exp(scores - row_top)
        attention = (exponent / lax.optimization_barrier(jnp.sum(exponent, axis=-1, keepdims=True))).astype(jnp.bfloat16)
        output = jnp.einsum('kgij,jkd->ikgd', attention.astype(jnp.float32), value_block).astype(jnp.bfloat16).reshape(TOK_DEV, HEADS * HD)
        grad_block = lax.dynamic_slice_in_dim(attn_grad, first_row, TOK_DEV, 0).astype(jnp.float32).reshape(TOK_DEV, KV_HEADS, group_size, HD)
        term = jnp.einsum('kgij,ikgd->jkd', attention.astype(jnp.float32), grad_block).reshape(4 * TOK_DEV, kv_width)
        current = lax.dynamic_slice_in_dim(carried, first_row, 4 * TOK_DEV, 0)
        carried = lax.dynamic_update_slice_in_dim(carried, current + term, first_row, 0)
        return (carried, output)
    carried, outputs = lax.scan(block_step, jnp.zeros((TOKENS + front_pad, kv_width), jnp.float32), jnp.arange(N_CTX, dtype=jnp.int32))
    attention_output_rows = outputs.reshape(TOKENS, HEADS * HD)
    value_gradient_rows = carried[front_pad:].astype(jnp.bfloat16)
    output_down_rows = jnp.dot(attention_output_rows, adapter_a_o, preferred_element_type=jnp.float32).astype(jnp.bfloat16)
    output_adapter_term = (ADAPTER_SCALE * jnp.dot(output_down_rows, output_up_matrix, preferred_element_type=jnp.float32)).astype(jnp.bfloat16)
    value_down_row_gradient = (ADAPTER_SCALE * jnp.dot(value_gradient_rows, value_up_matrix.T, preferred_element_type=jnp.float32)).astype(jnp.bfloat16)
    input_adapter_gradient = jnp.dot(value_down_row_gradient, adapter_a_v.T, preferred_element_type=jnp.float32).astype(jnp.bfloat16)
    value_down_gradient = jnp.dot(hidden.T, value_down_row_gradient, preferred_element_type=jnp.float32)
    value_up_gradient = ADAPTER_SCALE * jnp.dot(value_down_rows.T, value_gradient_rows, preferred_element_type=jnp.float32)
    output_down_gradient = jnp.dot(attention_output_rows.T, output_down_row_gradient, preferred_element_type=jnp.float32)
    output_up_gradient = ADAPTER_SCALE * jnp.dot(output_down_rows.T, output_gradient_rows, preferred_element_type=jnp.float32)
    return (attention_output_rows, output_adapter_term, input_adapter_gradient, value_down_gradient, value_up_gradient, output_down_gradient, output_up_gradient)
```

```python
import functools
import math

import jax
import jax.numpy as jnp
from jax import lax
from jax.experimental import pallas as pl
from jax.experimental.pallas import tpu as pltpu
from jax.sharding import PartitionSpec as P

HD = 128
BETA = 0.5
NEG = -1e30
F32 = jnp.float32
BF16 = jnp.bfloat16
KB = 256


def shift(value, by):
    n = lax.axis_size("ctx")
    pairs = [(i, i + by) for i in range(n) if 0 <= i + by < n]
    return lax.ppermute(value, "ctx", pairs)


def flip(value, mask):
    n = lax.axis_size("ctx")
    return lax.ppermute(value, "ctx", [(i, i ^ mask) for i in range(n)])


def spread_margins(part):
    n_ctx, n_tp = lax.axis_size("ctx"), lax.axis_size("tp")
    per = n_ctx // n_tp
    total = None
    for m in range(per):
        pairs = [
            ((c ^ (per * j + m)) * n_tp + j, c * n_tp + j)
            for c in range(n_ctx)
            for j in range(n_tp)
        ]
        got = lax.ppermute(part, ("ctx", "tp"), pairs)
        total = got if total is None else total + got
    return total


def share_tp(rows):
    n = lax.axis_size("tp")
    return lax.all_to_all(jnp.broadcast_to(rows[None], (n,) + rows.shape), "tp", 0, 0)


def nt(left, right):
    return lax.dot_general(left, right, (((1,), (1,)), ((), ())), preferred_element_type=F32)


def nn(left, right):
    return lax.dot_general(left, right, (((1,), (0,)), ((), ())), preferred_element_type=F32)


def tn(left, right):
    return lax.dot_general(left, right, (((0,), (0,)), ((), ())), preferred_element_type=F32)


def attn_kernel(
    start_ref, q_ref, g_ref, aot_ref, r_ref, k0, k1, k2, k3, v0, v1, v2, v3, lv_ref, uvt_ref, uv_ref,
    o_ref, lowo_ref, z_ref, vg_ref,
    bias, vt, s_scr, p_scr, vg,
):
    head = pl.program_id(0)
    rows = q_ref.shape[0]
    width = 4 * rows
    n_kb = width // KB
    scale = math.log2(math.e) / math.sqrt(HD)
    ks = (k0, k1, k2, k3)
    per = rows // KB

    @pl.when(head == 0)
    def _():
        start = start_ref[0:1, :]
        qpos = start_ref[1:2, :]
        for kb in range(n_kb):
            kpos = lax.broadcasted_iota(jnp.int32, (KB, rows), 0) + kb * KB
            ok = (kpos >= start) & (kpos <= qpos)
            bias[kb * KB : (kb + 1) * KB, :] = jnp.where(ok, 0.0, NEG)
        for s, ref in enumerate((v0, v1, v2, v3)):
            low = lv_ref[:, s * rows : (s + 1) * rows]
            frozen = ref[...].astype(F32).T
            vt[:, s * rows : (s + 1) * rows] = (frozen + 2.0 * nn(uvt_ref[...], low)).astype(BF16)
        vg[...] = jnp.zeros_like(vg)
        lowo_ref[...] = jnp.zeros_like(lowo_ref)

    q = q_ref[...]
    top = None
    for kb in range(n_kb):
        key = ks[kb // per][(kb % per) * KB : (kb % per + 1) * KB, :]
        s = nt(key, q) * scale + bias[kb * KB : (kb + 1) * KB, :]
        s_scr[kb * KB : (kb + 1) * KB, :] = s
        m = jnp.max(s, axis=0, keepdims=True)
        top = m if top is None else jnp.maximum(top, m)
    total = None
    for kb in range(n_kb):
        e = jnp.exp2(s_scr[kb * KB : (kb + 1) * KB, :] - top)
        p_scr[kb * KB : (kb + 1) * KB, :] = e.astype(BF16)
        m = jnp.sum(e, axis=0, keepdims=True)
        total = m if total is None else total + m
    inv = 1.0 / total
    ot = (nn(vt[...], p_scr[...]) * inv).astype(BF16)
    o_ref[...] = ot.astype(F32).T.astype(BF16)
    lowo_ref[...] += nn(aot_ref[...], ot)
    inv_rows = jnp.broadcast_to(inv, (HD, rows)).T
    grad = g_ref[...].astype(F32) + nn(r_ref[...], aot_ref[...])
    grad = (grad * inv_rows).astype(BF16)
    vg[...] += nn(p_scr[...], grad)

    @pl.when(head == pl.num_programs(0) - 1)
    def _():
        total_vg = vg[...].astype(BF16)
        vg_ref[...] = total_vg
        z_ref[...] = nt(uv_ref[...], total_vg).astype(BF16)


def attention(start_q, queries, cotangent, a_o_t, r, keys, frozen, low_v_t, u_v):
    rows = queries.shape[0]
    heads = queries.shape[1] // HD
    rank = u_v.shape[0]
    full = lambda shape: pl.BlockSpec(shape, lambda h: (0, 0))
    column = pl.BlockSpec((rows, HD), lambda h: (0, h))
    return pl.pallas_call(
        attn_kernel,
        grid=(heads,),
        in_specs=[full(start_q.shape), column, column, pl.BlockSpec((rank, HD), lambda h: (0, h)), full(r.shape)]
        + [full((rows, HD))] * 8
        + [full(low_v_t.shape), full((HD, rank)), full((rank, HD))],
        out_specs=[column, full((rank, rows)), full((rank, 4 * rows)), full((4 * rows, HD))],
        out_shape=[
            jax.ShapeDtypeStruct((rows, heads * HD), BF16),
            jax.ShapeDtypeStruct((rank, rows), F32),
            jax.ShapeDtypeStruct((rank, 4 * rows), BF16),
            jax.ShapeDtypeStruct((4 * rows, HD), BF16),
        ],
        scratch_shapes=[
            pltpu.VMEM((4 * rows, rows), F32),
            pltpu.VMEM((HD, 4 * rows), BF16),
            pltpu.VMEM((4 * rows, rows), F32),
            pltpu.VMEM((4 * rows, rows), BF16),
            pltpu.VMEM((4 * rows, HD), F32),
        ],
        compiler_params=pltpu.CompilerParams(
            dimension_semantics=("arbitrary",), vmem_limit_bytes=48 * 2**20
        ),
        name="attn",
    )(start_q, queries, cotangent, a_o_t, r, *keys, *frozen, low_v_t, u_v.T, u_v)


def grads_kernel(
    shared_ref, pair_ref, ends_ref, rt_ref, lv_ref, vg_ref, hidden_ref, o_ref, dout_ref,
    vd_ref, od_ref, ou_ref, vu_ref, lowo_ref, lvg_ref, wr_scr, wlo_scr,
):
    step = pl.program_id(0)
    rank, rows = rt_ref.shape
    width = lv_ref.shape[1]

    @pl.when(step == 0)
    def _():
        sums = shared_ref[0].astype(F32)
        for j in range(1, shared_ref.shape[0]):
            sums = sums + shared_ref[j].astype(F32)
        line = sums[2 * rank : 2 * rank + 1, :]
        margin = line[:, 0:128] + line[:, 128:256] + line[:, 256:384]
        gap = jnp.sum(pair_ref[:, 0:128] * margin, axis=1, keepdims=True)
        sign = pair_ref[:, 128:129]
        weight = -BETA * sign / (1.0 + jnp.exp(BETA * gap))
        docs = weight.shape[0]
        token = lax.broadcasted_iota(jnp.int32, (docs, width), 1)
        inside = (token >= ends_ref[:, 0:1]) & (token < ends_ref[:, 1:2])
        token_weight = jnp.sum(jnp.where(inside, weight, 0.0), axis=0, keepdims=True)
        own = token_weight[:, width - rows :]
        lvg_ref[...] = (2.0 * own * sums[0:rank]).astype(BF16)
        low_o = sums[rank : 2 * rank].astype(BF16)
        lowo_ref[...] = low_o
        wr_scr[...] = (own * rt_ref[...].astype(F32)).astype(BF16)
        wlo_scr[...] = (own * low_o.astype(F32)).astype(BF16)
        wlv = (token_weight * lv_ref[...].astype(F32)).astype(BF16)
        vu_ref[...] = (2.0 * nn(wlv, vg_ref[...])).astype(BF16)

    vd_ref[...] = nn(lvg_ref[...], hidden_ref[...]).astype(BF16)
    od_ref[...] = nn(wr_scr[...], o_ref[...]).astype(BF16)
    ou_ref[...] = (2.0 * nn(wlo_scr[...], dout_ref[...])).astype(BF16)


def grads(shared, pair, ends, r_t, low_v_t, vg, hidden, o, d_out):
    rank, rows = r_t.shape
    cols = hidden.shape[1]
    tile = min(256, cols)
    full = lambda a: pl.BlockSpec(a.shape, lambda i: (0,) * a.ndim)
    column = pl.BlockSpec((rows, tile), lambda i: (0, i))
    part = pl.BlockSpec((rank, tile), lambda i: (0, i))
    small = pl.BlockSpec((rank, rows), lambda i: (0, 0))
    return pl.pallas_call(
        grads_kernel,
        grid=(cols // tile,),
        in_specs=[full(a) for a in (shared, pair, ends, r_t, low_v_t, vg)] + [column] * 3,
        out_specs=[part, part, part, pl.BlockSpec((rank, HD), lambda i: (0, 0)), small, small],
        out_shape=[jax.ShapeDtypeStruct((rank, cols), BF16)] * 3
        + [jax.ShapeDtypeStruct((rank, HD), BF16)]
        + [jax.ShapeDtypeStruct((rank, rows), BF16)] * 2,
        scratch_shapes=[pltpu.VMEM((rank, rows), BF16)] * 2,
        compiler_params=pltpu.CompilerParams(
            dimension_semantics=("arbitrary",), vmem_limit_bytes=32 * 2**20
        ),
        name="grads",
    )(shared, pair, ends, r_t, low_v_t, vg, hidden, o, d_out)


def three_parts(x):
    keep = functools.partial(lax.reduce_precision, exponent_bits=8, mantissa_bits=7)
    high = keep(x)
    mid = keep(x - high)
    return high, mid, x - high - mid


def shards(
    hidden, queries, rotated_keys, frozen_value_rows, adapter_a_v, value_up_matrix, adapter_a_o,
    output_up_matrix, doc_lengths, pair_slots, token_logratio, out_cotangent, attn_cotangent,
):
    rows = hidden.shape[0]
    rank = value_up_matrix.shape[0]
    docs = doc_lengths.shape[0]
    first = lax.axis_index("ctx") * rows

    kv = jnp.concatenate([rotated_keys, frozen_value_rows], axis=0)
    kv_behind = [shift(kv, by) for by in (3, 2, 1)]
    keys = [x[:rows] for x in kv_behind] + [rotated_keys]
    frozen = [x[rows:] for x in kv_behind] + [frozen_value_rows]

    low_v_part = lax.dot_general(
        adapter_a_v, hidden, (((0,), (1,)), ((), ())), preferred_element_type=F32
    )
    r_part = nt(output_up_matrix, out_cotangent)
    stacked = jnp.concatenate([low_v_part, r_part], axis=0).astype(BF16)
    shared = jnp.sum(share_tp(stacked).astype(F32), axis=0)
    low_v_t = shared[:rank].astype(BF16)
    r_t = (2.0 * shared[rank:]).astype(BF16)
    low_v_window = jnp.concatenate([shift(low_v_t, by) for by in (3, 2, 1)] + [low_v_t], axis=1)

    doc_ids = jnp.arange(docs, dtype=jnp.int32)
    upto = (doc_ids[:, None] <= doc_ids[None, :]).astype(jnp.int32)
    doc_ends = jnp.sum(upto * doc_lengths[:, None], axis=0)
    doc_starts = doc_ends - doc_lengths
    pos = first + jnp.arange(rows, dtype=jnp.int32)
    own = (doc_starts[:, None] <= pos[None, :]) & (pos[None, :] < doc_ends[:, None])
    margin_part = jnp.sum(jnp.where(own, token_logratio[None, :], 0.0), axis=1)
    margin_part = spread_margins(margin_part)
    base = first - 3 * rows
    start = jnp.sum(jnp.where(own, doc_starts[:, None], 0), axis=0) - base
    start_q = jnp.zeros((8, rows), jnp.int32).at[0].set(start).at[1].set(pos - base)

    o, low_o_part, z, vg = attention(
        start_q, queries, attn_cotangent, adapter_a_o.T, r_t.T, keys, frozen, low_v_window, value_up_matrix
    )

    z_own = z[:, 3 * rows :].astype(F32)
    for slot in range(3):
        z_own = z_own + shift(z[:, slot * rows : (slot + 1) * rows], slot - 3).astype(F32)
    line = jnp.zeros((1, rows), F32)
    for i, piece in enumerate(three_parts(margin_part)):
        line = lax.dynamic_update_slice(line, piece[None, :], (0, 128 * i))
    line = jnp.pad(line, ((0, 7), (0, 0)))
    sent = jnp.concatenate([z_own, low_o_part, line], axis=0).astype(BF16)
    shared_back = share_tp(sent)

    pair_ids = pair_slots // 2
    sign = jnp.where(pair_slots % 2 == 0, 1.0, -1.0).astype(F32)
    pair = jnp.where(pair_ids[:, None] == pair_ids[None, :], sign[None, :], 0.0)
    pair = jnp.concatenate(
        [jnp.pad(pair, ((0, 0), (0, 128 - docs))), jnp.broadcast_to(sign[:, None], (docs, 128))], axis=1
    )
    ends = jnp.stack([doc_starts - base, doc_ends - base], axis=1)
    ends = jnp.pad(ends, ((0, 0), (0, 126)))
    vd, od, ou, vu, low_o_t, lvg_t = grads(
        shared_back, pair, ends, r_t, low_v_window, vg, hidden, o, out_cotangent
    )
    total = jnp.concatenate([vd, od, ou, vu], axis=1).astype(F32)
    for mask in (1, 2, 4, 8, 16):
        total = total + flip(total.astype(BF16), mask).astype(F32)
    cols = hidden.shape[1]
    term = (2.0 * tn(low_o_t, output_up_matrix)).astype(BF16)
    input_grad = lax.dot_general(
        lvg_t, adapter_a_v, (((0,), (1,)), ((), ())), preferred_element_type=F32
    ).astype(BF16)
    return (
        o,
        term,
        input_grad,
        total[:, :cols].T,
        total[:, 3 * cols :],
        total[:, cols : 2 * cols].T,
        total[:, 2 * cols : 3 * cols],
    )


def solution(mesh):
    both, tp_rows, tp_cols = P("ctx", "tp"), P("tp", None), P(None, "tp")
    in_specs = (
        both, both, both, both, tp_rows, tp_cols, tp_rows, tp_cols, P(), P(), P("ctx"), both, both,
    )
    out_specs = (both, both, both, tp_rows, tp_cols, tp_rows, tp_cols)
    return jax.shard_map(shards, mesh=mesh, in_specs=in_specs, out_specs=out_specs, check_vma=False)
```

```python
import functools
import math

import jax
import jax.numpy as jnp
from jax import lax
from jax.experimental import pallas as pl
from jax.experimental.pallas import tpu as pltpu
from jax.sharding import PartitionSpec as P

HD = 128
BETA = 0.5
NEG = -1e30
F32 = jnp.float32
BF16 = jnp.bfloat16
KB = 256


def shift(value, by):
    n = lax.axis_size("ctx")
    return lax.ppermute(value, "ctx", [(i, (i + by) % n) for i in range(n)])


def flip(value, mask):
    n = lax.axis_size("ctx")
    return lax.ppermute(value, "ctx", [(i, i ^ mask) for i in range(n)])


def spread(part):
    n_ctx, n_tp = lax.axis_size("ctx"), lax.axis_size("tp")
    per = n_ctx // n_tp
    pairs = [
        ((c + per * j) % n_ctx * n_tp + j, c * n_tp + j) for c in range(n_ctx) for j in range(n_tp)
    ]
    return lax.ppermute(part, ("ctx", "tp"), pairs)


def share_tp(rows):
    n = lax.axis_size("tp")
    return lax.all_to_all(jnp.broadcast_to(rows[None], (n,) + rows.shape), "tp", 0, 0)


def nt(left, right):
    return lax.dot_general(left, right, (((1,), (1,)), ((), ())), preferred_element_type=F32)


def nn(left, right):
    return lax.dot_general(left, right, (((1,), (0,)), ((), ())), preferred_element_type=F32)


def tn(left, right):
    return lax.dot_general(left, right, (((0,), (0,)), ((), ())), preferred_element_type=F32)


def attn_kernel(
    start_ref, q_ref, g_ref, aot_ref, rt_ref, kv0, kv1, kv2, kv3, lv_far, lv_near, lv_own, uvt_ref, uv_ref,
    o_ref, lowo_ref, z_ref, vg_ref,
    kv, sems, bias, vt, r_scr, s_scr, p_scr, vg,
):
    head = pl.program_id(0)
    rows = q_ref.shape[0]
    rank = uv_ref.shape[0]
    width = 4 * rows
    n_kb = width // KB
    scale = math.log2(math.e) / math.sqrt(HD)
    per = rows // KB

    @pl.when(head == 0)
    def _():
        copies = [
            pltpu.make_async_copy(ref, kv.at[slot], sems.at[slot])
            for slot, ref in enumerate((kv0, kv1, kv2, kv3))
        ]
        for copy in copies:
            copy.start()
        start = start_ref[0:1, :]
        qpos = start_ref[1:2, :]
        for kb in range(n_kb):
            kpos = lax.broadcasted_iota(jnp.int32, (KB, rows), 0) + kb * KB
            ok = (kpos >= start) & (kpos <= qpos)
            bias[kb * KB : (kb + 1) * KB, :] = jnp.where(ok, 0.0, NEG)
        r_scr[...] = rt_ref[...].astype(F32).T.astype(BF16)
        vg[...] = jnp.zeros_like(vg)
        lowo_ref[...] = jnp.zeros_like(lowo_ref)
        lows = (
            lv_far[0:rank, 0:rows], lv_far[0:rank, rows : 2 * rows], lv_near[0:rank, :], lv_own[0:rank, :],
        )
        for slot, copy in enumerate(copies):
            copy.wait()
            frozen = kv[slot, rows : 2 * rows, :].astype(F32).T
            vt[:, slot * rows : (slot + 1) * rows] = (frozen + 2.0 * nn(uvt_ref[...], lows[slot])).astype(BF16)

    q = q_ref[...]
    top = None
    for kb in range(n_kb):
        key = kv[kb // per, (kb % per) * KB : (kb % per + 1) * KB, :]
        s = nt(key, q) * scale + bias[kb * KB : (kb + 1) * KB, :]
        s_scr[kb * KB : (kb + 1) * KB, :] = s
        m = jnp.max(s, axis=0, keepdims=True)
        top = m if top is None else jnp.maximum(top, m)
    total = None
    for kb in range(n_kb):
        e = jnp.exp2(s_scr[kb * KB : (kb + 1) * KB, :] - top)
        p_scr[kb * KB : (kb + 1) * KB, :] = e.astype(BF16)
        m = jnp.sum(e, axis=0, keepdims=True)
        total = m if total is None else total + m
    inv = 1.0 / total
    ot = (nn(vt[...], p_scr[...]) * inv).astype(BF16)
    o_ref[...] = ot.astype(F32).T.astype(BF16)
    lowo_ref[...] += nn(aot_ref[...], ot)
    inv_rows = jnp.broadcast_to(inv, (HD, rows)).T
    grad = g_ref[...].astype(F32) + nn(r_scr[...], aot_ref[...])
    grad = (grad * inv_rows).astype(BF16)
    vg[...] += nn(p_scr[...], grad)

    @pl.when(head == pl.num_programs(0) - 1)
    def _():
        total_vg = vg[...].astype(BF16)
        vg_ref[...] = total_vg
        z_ref[...] = nt(uv_ref[...], total_vg).astype(BF16)


def attention(start_q, queries, cotangent, a_o_t, r_t, kvs, lows, u_v):
    rows = queries.shape[0]
    heads = queries.shape[1] // HD
    rank = u_v.shape[0]
    full = lambda shape: pl.BlockSpec(shape, lambda h: (0, 0))
    column = pl.BlockSpec((rows, HD), lambda h: (0, h))
    return pl.pallas_call(
        attn_kernel,
        grid=(heads,),
        in_specs=[full(start_q.shape), column, column, pl.BlockSpec((rank, HD), lambda h: (0, h)), full(r_t.shape)]
        + [pl.BlockSpec(memory_space=pl.ANY)] * 4
        + [full(a.shape) for a in lows]
        + [full((HD, rank)), full((rank, HD))],
        out_specs=[column, full((rank, rows)), full((rank, 4 * rows)), full((4 * rows, HD))],
        out_shape=[
            jax.ShapeDtypeStruct((rows, heads * HD), BF16),
            jax.ShapeDtypeStruct((rank, rows), F32),
            jax.ShapeDtypeStruct((rank, 4 * rows), BF16),
            jax.ShapeDtypeStruct((4 * rows, HD), BF16),
        ],
        scratch_shapes=[
            pltpu.VMEM((4, 2 * rows, HD), BF16),
            pltpu.SemaphoreType.DMA((4,)),
            pltpu.VMEM((4 * rows, rows), F32),
            pltpu.VMEM((HD, 4 * rows), BF16),
            pltpu.VMEM((rows, rank), BF16),
            pltpu.VMEM((4 * rows, rows), F32),
            pltpu.VMEM((4 * rows, rows), BF16),
            pltpu.VMEM((4 * rows, HD), F32),
        ],
        compiler_params=pltpu.CompilerParams(
            dimension_semantics=("arbitrary",), vmem_limit_bytes=48 * 2**20
        ),
        name="attn",
    )(start_q, queries, cotangent, a_o_t, r_t, *kvs, *lows, u_v.T, u_v)


def grads_kernel(
    shared_ref, pair_ref, ends_ref, rt_ref, lv_far, lv_near, lv_own, vg_ref, hidden_ref, o_ref, dout_ref,
    vd_ref, od_ref, ou_ref, vu_ref, lowo_ref, lvg_ref, wr_scr, wlo_scr,
):
    step = pl.program_id(0)
    rank, rows = rt_ref.shape
    width = vg_ref.shape[0]

    @pl.when(step == 0)
    def _():
        sums = shared_ref[0].astype(F32)
        for j in range(1, shared_ref.shape[0]):
            sums = sums + shared_ref[j].astype(F32)
        line = sums[2 * rank : 2 * rank + 1, :]
        margin = line[:, 0:128] + line[:, 128:256] + line[:, 256:384]
        gap = jnp.sum(pair_ref[:, 0:128] * margin, axis=1, keepdims=True)
        sign = pair_ref[:, 128:129]
        weight = -BETA * sign / (1.0 + jnp.exp(BETA * gap))
        docs = weight.shape[0]
        token = lax.broadcasted_iota(jnp.int32, (docs, width), 1)
        inside = (token >= ends_ref[:, 0:1]) & (token < ends_ref[:, 1:2])
        token_weight = jnp.sum(jnp.where(inside, weight, 0.0), axis=0, keepdims=True)
        own = token_weight[:, width - rows :]
        lvg_ref[...] = (2.0 * own * sums[0:rank]).astype(BF16)
        low_o = sums[rank : 2 * rank].astype(BF16)
        lowo_ref[...] = low_o
        wr_scr[...] = (own * rt_ref[...].astype(F32)).astype(BF16)
        wlo_scr[...] = (own * low_o.astype(F32)).astype(BF16)
        up = jnp.zeros(vu_ref.shape, F32)
        for ref, at in ((lv_far, 0), (lv_near, 2 * rows), (lv_own, 3 * rows)):
            end = at + ref.shape[1]
            wlv = (token_weight[:, at:end] * ref[0:rank, :].astype(F32)).astype(BF16)
            up = up + nn(wlv, vg_ref[at:end, :])
        vu_ref[...] = (2.0 * up).astype(BF16)

    vd_ref[...] = nn(lvg_ref[...], hidden_ref[...]).astype(BF16)
    od_ref[...] = nn(wr_scr[...], o_ref[...]).astype(BF16)
    ou_ref[...] = (2.0 * nn(wlo_scr[...], dout_ref[...])).astype(BF16)


def grads(shared, pair, ends, r_t, lows, vg, hidden, o, d_out):
    rank, rows = r_t.shape
    cols = hidden.shape[1]
    tile = min(256, cols)
    full = lambda a: pl.BlockSpec(a.shape, lambda i: (0,) * a.ndim)
    column = pl.BlockSpec((rows, tile), lambda i: (0, i))
    part = pl.BlockSpec((rank, tile), lambda i: (0, i))
    small = pl.BlockSpec((rank, rows), lambda i: (0, 0))
    return pl.pallas_call(
        grads_kernel,
        grid=(cols // tile,),
        in_specs=[full(a) for a in (shared, pair, ends, r_t, *lows, vg)] + [column] * 3,
        out_specs=[part, part, part, pl.BlockSpec((rank, HD), lambda i: (0, 0)), small, small],
        out_shape=[jax.ShapeDtypeStruct((rank, cols), BF16)] * 3
        + [jax.ShapeDtypeStruct((rank, HD), BF16)]
        + [jax.ShapeDtypeStruct((rank, rows), BF16)] * 2,
        scratch_shapes=[pltpu.VMEM((rank, rows), BF16)] * 2,
        compiler_params=pltpu.CompilerParams(
            dimension_semantics=("arbitrary",), vmem_limit_bytes=32 * 2**20
        ),
        name="grads",
    )(shared, pair, ends, r_t, *lows, vg, hidden, o, d_out)


def three_parts(x):
    keep = functools.partial(lax.reduce_precision, exponent_bits=8, mantissa_bits=7)
    high = keep(x)
    mid = keep(x - high)
    return high, mid, x - high - mid


def margin_rows(margin, width):
    line = [jnp.pad(part, (0, 128 - part.shape[0])) for part in three_parts(margin)]
    line = jnp.concatenate(line + [jnp.zeros((width - 384,), F32)])
    return jnp.pad(line[None, :], ((0, 7), (0, 0)))


def margin_of(line):
    line = line.astype(F32)
    return line[0:128] + line[128:256] + line[256:384]


def shards(
    hidden, queries, rotated_keys, frozen_value_rows, adapter_a_v, value_up_matrix, adapter_a_o,
    output_up_matrix, doc_lengths, pair_slots, token_logratio, out_cotangent, attn_cotangent,
):
    rows = hidden.shape[0]
    rank = value_up_matrix.shape[0]
    docs = doc_lengths.shape[0]
    first = lax.axis_index("ctx") * rows

    kv = jnp.concatenate([rotated_keys, frozen_value_rows], axis=0)
    kvs = [shift(kv, by) for by in (3, 2, 1)]

    low_v_part = lax.dot_general(
        adapter_a_v, hidden, (((0,), (1,)), ((), ())), preferred_element_type=F32
    )
    r_part = nt(output_up_matrix, out_cotangent)
    stacked = jnp.concatenate([low_v_part, r_part], axis=0).astype(BF16)
    shared = jnp.sum(share_tp(stacked).astype(F32), axis=0)
    r_t = (2.0 * shared[rank:]).astype(BF16)

    doc_ids = jnp.arange(docs, dtype=jnp.int32)
    upto = (doc_ids[:, None] <= doc_ids[None, :]).astype(jnp.int32)
    doc_ends = jnp.sum(upto * doc_lengths[:, None], axis=0)
    doc_starts = doc_ends - doc_lengths
    pos = first + jnp.arange(rows, dtype=jnp.int32)
    own = (doc_starts[:, None] <= pos[None, :]) & (pos[None, :] < doc_ends[:, None])
    margin = jnp.sum(jnp.where(own, token_logratio[None, :], 0.0), axis=1)
    base = first - 3 * rows
    start = jnp.sum(jnp.where(own, doc_starts[:, None], 0), axis=0) - base
    start_q = jnp.zeros((8, rows), jnp.int32).at[0].set(start).at[1].set(pos - base)

    low_own = jnp.concatenate([shared[:rank], margin_rows(margin, rows)], axis=0).astype(BF16)
    low_own, kvs = lax.optimization_barrier((low_own, kvs))
    low_near = shift(low_own, 1)
    low_far = shift(jnp.concatenate([low_near, low_own], axis=1), 2)
    lows = (low_far, low_near, low_own)

    o, low_o_part, z, vg = attention(
        start_q, queries, attn_cotangent, adapter_a_o.T, r_t, kvs + [kv], lows, value_up_matrix
    )

    margin = margin_of(low_own[rank]) + margin_of(low_near[rank])
    margin = margin + margin_of(low_far[rank, :rows]) + margin_of(low_far[rank, rows:])
    margin = spread(margin)
    z_far = shift(z[:, : 2 * rows], -2).astype(F32)
    z_near = shift((z[:, 2 * rows : 3 * rows].astype(F32) + z_far[:, :rows]).astype(BF16), -1)
    z_own = z[:, 3 * rows :].astype(F32) + z_far[:, rows:] + z_near.astype(F32)
    sent = jnp.concatenate([z_own, low_o_part, margin_rows(margin, rows)], axis=0).astype(BF16)
    shared_back = share_tp(sent)

    pair_ids = pair_slots // 2
    sign = jnp.where(pair_slots % 2 == 0, 1.0, -1.0).astype(F32)
    pair = jnp.where(pair_ids[:, None] == pair_ids[None, :], sign[None, :], 0.0)
    pair = jnp.concatenate(
        [jnp.pad(pair, ((0, 0), (0, 128 - docs))), jnp.broadcast_to(sign[:, None], (docs, 128))], axis=1
    )
    ends = jnp.stack([doc_starts - base, doc_ends - base], axis=1)
    ends = jnp.pad(ends, ((0, 0), (0, 126)))
    vd, od, ou, vu, low_o_t, lvg_t = grads(
        shared_back, pair, ends, r_t, lows, vg, hidden, o, out_cotangent
    )
    total = jnp.concatenate([vd, od, ou, vu], axis=1).astype(F32)
    for mask in (1, 2, 4, 8, 16):
        total = lax.reduce_precision(total, 8, 7)
        total = total + flip(total.astype(BF16), mask).astype(F32)
    cols = hidden.shape[1]
    term = (2.0 * tn(low_o_t, output_up_matrix)).astype(BF16)
    input_grad = lax.dot_general(
        lvg_t, adapter_a_v, (((0,), (1,)), ((), ())), preferred_element_type=F32
    ).astype(BF16)
    return (
        o,
        term,
        input_grad,
        total[:, :cols].T,
        total[:, 3 * cols :],
        total[:, cols : 2 * cols].T,
        total[:, 2 * cols : 3 * cols],
    )


def solution(mesh):
    both, tp_rows, tp_cols = P("ctx", "tp"), P("tp", None), P(None, "tp")
    in_specs = (
        both, both, both, both, tp_rows, tp_cols, tp_rows, tp_cols, P(), P(), P("ctx"), both, both,
    )
    out_specs = (both, both, both, tp_rows, tp_cols, tp_rows, tp_cols)
    return jax.shard_map(shards, mesh=mesh, in_specs=in_specs, out_specs=out_specs, check_vma=False)
```

```python
import math

import jax
import jax.numpy as jnp
from jax import lax
from jax.experimental import pallas as pl
from jax.experimental.pallas import tpu as pltpu
from jax.sharding import PartitionSpec as P

HD = 128
BETA = 0.5
NEG = -1e30
F32 = jnp.float32
BF16 = jnp.bfloat16
KB = 256


def shift(value, by):
    n = lax.axis_size("ctx")
    return lax.ppermute(value, "ctx", [(i, (i + by) % n) for i in range(n)])


def flip(value, mask):
    n = lax.axis_size("ctx")
    return lax.ppermute(value, "ctx", [(i, i ^ mask) for i in range(n)])


def spread(part):
    n_ctx, n_tp = lax.axis_size("ctx"), lax.axis_size("tp")
    per = n_ctx // n_tp
    pairs = [
        ((c + per * j) % n_ctx * n_tp + j, c * n_tp + j) for c in range(n_ctx) for j in range(n_tp)
    ]
    return lax.ppermute(part, ("ctx", "tp"), pairs)


def share_tp(rows):
    n = lax.axis_size("tp")
    return lax.all_to_all(jnp.broadcast_to(rows[None], (n,) + rows.shape), "tp", 0, 0)


def nt(left, right):
    return lax.dot_general(left, right, (((1,), (1,)), ((), ())), preferred_element_type=F32)


def nn(left, right):
    return lax.dot_general(left, right, (((1,), (0,)), ((), ())), preferred_element_type=F32)


def tn(left, right):
    return lax.dot_general(left, right, (((0,), (0,)), ((), ())), preferred_element_type=F32)


def three_parts(x):
    high = x.astype(BF16)
    rest = x - high.astype(F32)
    mid = rest.astype(BF16)
    return high, mid, (rest - mid.astype(F32)).astype(BF16)


def iota(shape, dim):
    return lax.broadcasted_iota(jnp.int32, shape, dim)


def column(row, count):
    shape = (count, row.shape[1])
    return jnp.sum(jnp.where(iota(shape, 0) == iota(shape, 1), row, 0), axis=1, keepdims=True)


def doc_bounds(len_row):
    docs = len_row.shape[1]
    shape = (docs, docs)
    end = jnp.sum(jnp.where(iota(shape, 1) <= iota(shape, 0), len_row, 0), axis=1, keepdims=True)
    return end - column(len_row, docs), end


def in_hbm(*arrays):
    return [pltpu.with_memory_space_constraint(a, pltpu.HBM) for a in arrays]


def prep_kernel(
    first_ref, len_hbm, ratio_hbm, avt_hbm, up_hbm, key_hbm, frozen_hbm, hidden_hbm, dout_hbm,
    kv_ref, rank_ref, margin_ref, start_ref,
    len_ref, ratio_ref, avt_ref, up_ref, hidden_ref, dout_ref, sems,
):
    rows = key_hbm.shape[0]
    rank = up_ref.shape[0]
    pairs = [
        (len_hbm, len_ref), (ratio_hbm, ratio_ref), (avt_hbm, avt_ref), (up_hbm, up_ref),
        (hidden_hbm, hidden_ref), (dout_hbm, dout_ref),
        (key_hbm, kv_ref.at[0:rows]), (frozen_hbm, kv_ref.at[rows : 2 * rows]),
    ]
    copies = [pltpu.make_async_copy(src, dst, sems.at[i]) for i, (src, dst) in enumerate(pairs)]
    for copy in copies:
        copy.start()
    copies[0].wait()
    copies[1].wait()
    docs = len_ref.shape[1]
    first = first_ref[0]
    begin, end = doc_bounds(len_ref[...])
    pos = iota((1, rows), 1) + first
    own = (begin <= pos) & (pos < end)
    margin = jnp.sum(jnp.where(own, ratio_ref[...], 0.0), axis=1, keepdims=True)
    shape = (docs, 128)
    margin = jnp.sum(jnp.where(iota(shape, 0) == iota(shape, 1), margin, 0.0), axis=0, keepdims=True)
    margin = jnp.broadcast_to(margin, (8, 128))
    margin_ref[...] = jnp.zeros_like(margin_ref)
    for i, part in enumerate(three_parts(margin)):
        margin_ref[:, i * 128 : (i + 1) * 128] = part
    base = first - 3 * rows
    start = jnp.sum(jnp.where(own, begin, 0), axis=0, keepdims=True) - base
    start_ref[...] = jnp.where(iota(start_ref.shape, 0) == 0, start, pos - base)
    copies[2].wait()
    copies[4].wait()
    rank_ref[0:rank, :] = nt(hidden_ref[...], avt_ref[...]).T.astype(BF16)
    copies[3].wait()
    copies[5].wait()
    rank_ref[rank : 2 * rank, :] = nt(dout_ref[...], up_ref[...]).T.astype(BF16)
    copies[6].wait()
    copies[7].wait()


def prepare(first, doc_lengths, token_logratio, a_v_t, up, keys, frozen, hidden, d_out):
    rows = keys.shape[0]
    rank = up.shape[0]
    vmem = pl.BlockSpec(memory_space=pltpu.VMEM)
    return pl.pallas_call(
        prep_kernel,
        in_specs=[pl.BlockSpec(memory_space=pltpu.SMEM)] + [pl.BlockSpec(memory_space=pltpu.HBM)] * 8,
        out_specs=[vmem] * 4,
        out_shape=[
            jax.ShapeDtypeStruct((2 * rows, HD), BF16),
            jax.ShapeDtypeStruct((2 * rank, rows), BF16),
            jax.ShapeDtypeStruct((8, rows), BF16),
            jax.ShapeDtypeStruct((8, rows), jnp.int32),
        ],
        scratch_shapes=[
            pltpu.VMEM(a.shape, a.dtype)
            for a in (doc_lengths, token_logratio, a_v_t, up, hidden, d_out)
        ]
        + [pltpu.SemaphoreType.DMA((8,))],
        compiler_params=pltpu.CompilerParams(vmem_limit_bytes=32 * 2**20),
        name="prep",
    )(first, *in_hbm(doc_lengths, token_logratio, a_v_t, up, keys, frozen, hidden, d_out))


def margin_of(line):
    return line[:, 0:128] + line[:, 128:256] + line[:, 256:384]


def attn_kernel(
    low_ref, q_ref, g_ref, len_hbm, slot_hbm, aot_hbm, uv_hbm, start_hbm, rt_hbm, kv0, kv1, kv2, kv3, far_hbm, near_hbm, own_hbm,
    o_ref, lowo_ref, z_ref, vu_ref, od_ref, weight_ref,
    len_ref, slot_ref, aot_ref, uv_ref, start_ref, rt_ref, kv, lv_far, lv_near, lv_own, sems,
    bias0, bias1, vt, r_scr, q_all, s_scr, p_scr, ot_scr, grad_all, vg,
):
    rows = q_ref.shape[0]
    heads = q_ref.shape[1] // HD
    rank = uv_ref.shape[0]
    width = 4 * rows
    n_kb = width // KB
    scale = math.log2(math.e) / math.sqrt(HD)
    halves = rows // KB

    pairs = [
        (len_hbm, len_ref), (slot_hbm, slot_ref), (aot_hbm, aot_ref), (uv_hbm, uv_ref),
        (start_hbm, start_ref), (rt_hbm, rt_ref),
        (far_hbm, lv_far), (near_hbm, lv_near), (own_hbm, lv_own),
    ]
    pairs += [(ref, kv.at[slot]) for slot, ref in enumerate((kv0, kv1, kv2, kv3))]
    copies = [pltpu.make_async_copy(src, dst, sems.at[i]) for i, (src, dst) in enumerate(pairs)]
    for copy in copies:
        copy.start()
    vg[...] = jnp.zeros_like(vg)
    lowo_ref[...] = jnp.zeros_like(lowo_ref)
    for copy in copies:
        copy.wait()
    biases = (bias0, bias1)
    for half in range(halves):
        start = start_ref[0:1, half * KB : (half + 1) * KB]
        qpos = start_ref[1:2, half * KB : (half + 1) * KB]
        for kb in range(n_kb):
            kpos = iota((KB, KB), 0) + kb * KB
            ok = (kpos >= start) & (kpos <= qpos)
            biases[half][kb * KB : (kb + 1) * KB, :] = jnp.where(ok, 0.0, NEG)
    r_scr[...] = rt_ref[...].astype(F32).T.astype(BF16)
    uvt = uv_ref[...].astype(F32).T.astype(BF16)
    lows = (
        lv_far[0:rank, 0:rows], lv_far[0:rank, rows : 2 * rows], lv_near[0:rank, :], lv_own[0:rank, :],
    )
    lows = [low.astype(BF16) for low in lows]
    line = lv_far[rank : rank + 1, 0:rows] + lv_far[rank : rank + 1, rows : 2 * rows]
    margin = margin_of(line + lv_near[rank : rank + 1, :] + lv_own[rank : rank + 1, :])
    docs = len_ref.shape[1]
    slots = slot_ref[...]
    slot = column(slots, docs)
    sign = (1 - 2 * (slot & 1)).astype(F32)
    sign_row = (1 - 2 * (slots & 1)).astype(F32)
    pair = jnp.where((slot >> 1) == (slots >> 1), sign_row, 0.0)
    gap = jnp.sum(pair * margin[:, 0:docs], axis=1, keepdims=True)
    weight = -BETA * sign / (1.0 + jnp.exp(BETA * gap))
    begin, end = doc_bounds(len_ref[...])
    token = iota((docs, width), 1) + low_ref[halves]
    weight = jnp.sum(jnp.where((begin <= token) & (token < end), weight, 0.0), axis=0, keepdims=True)
    weight_ref[...] = jnp.broadcast_to(weight[:, 3 * rows :], weight_ref.shape)
    for slot in range(4):
        frozen = kv[slot, rows : 2 * rows, :].astype(F32).T
        v = (frozen + 2.0 * nn(uvt, lows[slot])).astype(BF16)
        for kb in range(halves):
            vt[slot * halves + kb] = v[:, kb * KB : (kb + 1) * KB]

    for half in range(halves):
        mine = slice(half * KB, (half + 1) * KB)
        first = low_ref[half]
        last = n_kb - halves + 1 + half
        lanes = [slice(h * KB, (h + 1) * KB) for h in range(heads)]
        for h in range(heads):
            q_all[h] = q_ref[mine, h * HD : (h + 1) * HD]

        def scores(kb, peaks):
            at = pl.ds(pl.multiple_of(kb * KB, KB), KB)
            key = kv[kb // halves, pl.ds(pl.multiple_of(kb % halves * KB, KB), KB), :]
            mask = biases[half][at, :]
            new = []
            for h in range(heads):
                s = nt(key, q_all[h]) * scale + mask
                s_scr[at, lanes[h]] = s
                new.append(jnp.maximum(peaks[h], jnp.max(s.reshape(KB // 8, 8, KB), axis=0)))
            return tuple(new)

        peaks = lax.fori_loop(first, last, scores, (jnp.full((8, KB), NEG, F32),) * heads)
        tops = [jnp.max(peak, axis=0, keepdims=True) for peak in peaks]
        ot_scr[...] = jnp.zeros_like(ot_scr)

        def probs(kb, totals):
            at = pl.ds(pl.multiple_of(kb * KB, KB), KB)
            new = []
            for h in range(heads):
                e = jnp.exp2(s_scr[at, lanes[h]] - tops[h])
                new.append(totals[h] + jnp.sum(e.reshape(KB // 8, 8, KB), axis=0))
                e = e.astype(BF16)
                p_scr[at, lanes[h]] = e
                ot_scr[:, lanes[h]] += nn(vt[kb], e)
            return tuple(new)

        totals = lax.fori_loop(first, last, probs, (jnp.zeros((8, KB), F32),) * heads)
        for h in range(heads):
            cols = slice(h * HD, (h + 1) * HD)
            inv = 1.0 / jnp.sum(totals[h], axis=0, keepdims=True)
            ot = (ot_scr[:, lanes[h]] * inv).astype(BF16)
            o_ref[mine, cols] = ot.astype(F32).T.astype(BF16)
            lowo_ref[:, mine] += nn(aot_ref[:, cols], ot)
            inv_rows = jnp.broadcast_to(inv, (HD, KB)).T
            grad = g_ref[mine, cols].astype(F32) + nn(r_scr[mine, :], aot_ref[:, cols])
            grad_all[lanes[h], :] = (grad * inv_rows).astype(BF16)

        def back(kb, carry):
            at = pl.ds(pl.multiple_of(kb * KB, KB), KB)
            vg[at, :] += nn(p_scr[at, :], grad_all[...])
            return carry

        lax.fori_loop(first, last, back, 0)

    total_vg = vg[...].astype(BF16)
    z_ref[...] = nt(uv_ref[...], total_vg).astype(BF16)
    up = jnp.zeros(vu_ref.shape, F32)
    for slot in range(4):
        part = slice(slot * rows, (slot + 1) * rows)
        up += nn((weight[:, part] * lows[slot].astype(F32)).astype(BF16), total_vg[part, :])
    vu_ref[...] = (2.0 * up).astype(BF16)
    weighted_r = (weight[:, 3 * rows :] * rt_ref[...].astype(F32)).astype(BF16)
    od_ref[...] = nn(weighted_r, o_ref[...]).astype(BF16)


def attention(base, start_q, queries, cotangent, doc_lengths, pair_slots, a_o_t, r_t, kvs, lows, u_v):
    rows = queries.shape[0]
    cols = queries.shape[1]
    rank = u_v.shape[0]
    heads = cols // HD
    halves = rows // KB
    low = jnp.stack([start_q[0, half * KB] for half in range(halves)]) // KB
    low = jnp.clip(low, 0, 3 * halves + jnp.arange(halves, dtype=jnp.int32))
    low = jnp.concatenate([low, base])
    vmem = pl.BlockSpec(memory_space=pltpu.VMEM)
    anywhere = pl.BlockSpec(memory_space=pl.ANY)
    hbm = pl.BlockSpec(memory_space=pltpu.HBM)
    args = (doc_lengths, pair_slots, a_o_t, u_v)
    made = (start_q, r_t)
    scratch = [pltpu.VMEM(a.shape, a.dtype) for a in args + made]
    scratch += [pltpu.VMEM((4, 2 * rows, HD), BF16)]
    scratch += [pltpu.VMEM(a.shape, a.dtype) for a in lows]
    return pl.pallas_call(
        attn_kernel,
        in_specs=[pl.BlockSpec(memory_space=pltpu.SMEM)] + [vmem] * 2 + [hbm] * 4 + [anywhere] * 9,
        out_specs=[vmem] * 6,
        out_shape=[
            jax.ShapeDtypeStruct((rows, cols), BF16),
            jax.ShapeDtypeStruct((rank, rows), F32),
            jax.ShapeDtypeStruct((rank, 4 * rows), BF16),
            jax.ShapeDtypeStruct((rank, HD), BF16),
            jax.ShapeDtypeStruct((rank, cols), BF16),
            jax.ShapeDtypeStruct((8, rows), F32),
        ],
        scratch_shapes=scratch
        + [
            pltpu.SemaphoreType.DMA((13,)),
            pltpu.VMEM((4 * rows, KB), F32),
            pltpu.VMEM((4 * rows, KB), F32),
            pltpu.VMEM((4 * halves, HD, KB), BF16),
            pltpu.VMEM((rows, rank), BF16),
            pltpu.VMEM((heads, KB, HD), BF16),
            pltpu.VMEM((4 * rows, heads * KB), F32),
            pltpu.VMEM((4 * rows, heads * KB), BF16),
            pltpu.VMEM((HD, heads * KB), F32),
            pltpu.VMEM((heads * KB, HD), BF16),
            pltpu.VMEM((4 * rows, HD), F32),
        ],
        compiler_params=pltpu.CompilerParams(vmem_limit_bytes=48 * 2**20),
        name="attn",
    )(low, queries, cotangent, *in_hbm(*args), *made, *kvs, *lows)


def grads_kernel(shared_ref, weight_ref, vu_ref, od_ref, hidden_ref, dout_ref, sum_ref, lowo_ref, lvg_ref):
    rank = vu_ref.shape[0]
    cols = hidden_ref.shape[1]
    sums = shared_ref[0].astype(F32)
    for j in range(1, shared_ref.shape[0]):
        sums = sums + shared_ref[j].astype(F32)
    own = weight_ref[0:1, :]
    lvg = (2.0 * own * sums[0:rank]).astype(BF16)
    low_o = sums[rank : 2 * rank].astype(BF16)
    lvg_ref[...] = lvg
    lowo_ref[...] = low_o
    sum_ref[:, 0:cols] = nn(lvg, hidden_ref[...]).astype(BF16)
    sum_ref[:, cols : 2 * cols] = od_ref[...]
    weighted = (own * low_o.astype(F32)).astype(BF16)
    sum_ref[:, 2 * cols : 3 * cols] = (2.0 * nn(weighted, dout_ref[...])).astype(BF16)
    sum_ref[:, 3 * cols :] = vu_ref[...]


def grads(shared, weight, vu, od, hidden, d_out):
    rank = vu.shape[0]
    rows, cols = hidden.shape
    vmem = pl.BlockSpec(memory_space=pltpu.VMEM)
    return pl.pallas_call(
        grads_kernel,
        in_specs=[vmem] * 6,
        out_specs=[vmem] * 3,
        out_shape=[
            jax.ShapeDtypeStruct((rank, 3 * cols + HD), BF16),
            jax.ShapeDtypeStruct((rank, rows), BF16),
            jax.ShapeDtypeStruct((rank, rows), BF16),
        ],
        compiler_params=pltpu.CompilerParams(vmem_limit_bytes=32 * 2**20),
        name="grads",
    )(shared, weight, vu, od, hidden, d_out)


def shards(
    hidden, queries, rotated_keys, frozen_value_rows, adapter_a_v, value_up_matrix, adapter_a_o,
    output_up_matrix, doc_lengths, pair_slots, token_logratio, out_cotangent, attn_cotangent,
):
    rows, cols = hidden.shape
    rank = value_up_matrix.shape[0]
    first = (lax.axis_index("ctx") * rows).astype(jnp.int32)[None]
    doc_lengths = doc_lengths[None, :]
    pair_slots = pair_slots[None, :]

    kv, rank_rows, margin, start_q = prepare(
        first, doc_lengths, token_logratio[None, :], adapter_a_v.T, output_up_matrix, rotated_keys,
        frozen_value_rows, hidden, out_cotangent,
    )
    kvs = [shift(kv, by) for by in (3, 2, 1)]
    sent = jnp.concatenate([rank_rows[:rank], spread(margin), rank_rows[rank:]], axis=0)
    shared = jnp.sum(share_tp(sent).astype(F32), axis=0)
    low_own = shared[: rank + 8]
    r_t = (2.0 * shared[rank + 8 :]).astype(BF16)
    low_own, kvs = lax.optimization_barrier((low_own, kvs))
    low_near = shift(low_own, 1)
    low_far = shift(jnp.concatenate([low_near, low_own], axis=1), 2)

    o, low_o_part, z, vu, od, weight = attention(
        first - 3 * rows, start_q, queries, attn_cotangent, doc_lengths, pair_slots, adapter_a_o.T, r_t,
        kvs + [kv], (low_far, low_near, low_own), value_up_matrix,
    )
    z_far = shift(z[:, : 2 * rows], -2).astype(F32)
    z_near = shift((z[:, 2 * rows : 3 * rows].astype(F32) + z_far[:, :rows]).astype(BF16), -1)
    z_own = z[:, 3 * rows :].astype(F32) + z_far[:, rows:] + z_near.astype(F32)
    shared_back = share_tp(jnp.concatenate([z_own, low_o_part], axis=0).astype(BF16))

    total, low_o_t, lvg_t = grads(shared_back, weight, vu, od, hidden, out_cotangent)
    total = total.astype(F32)
    for mask in (1, 2, 4, 8, 16):
        total = lax.reduce_precision(total, 8, 7)
        total = total + flip(total.astype(BF16), mask).astype(F32)
    term = (2.0 * tn(low_o_t, output_up_matrix)).astype(BF16)
    input_grad = lax.dot_general(
        lvg_t, adapter_a_v, (((0,), (1,)), ((), ())), preferred_element_type=F32
    ).astype(BF16)
    return (
        o,
        term,
        input_grad,
        total[:, :cols].T,
        total[:, 3 * cols :],
        total[:, cols : 2 * cols].T,
        total[:, 2 * cols : 3 * cols],
    )


def solution(mesh):
    both, tp_rows, tp_cols = P("ctx", "tp"), P("tp", None), P(None, "tp")
    in_specs = (
        both, both, both, both, tp_rows, tp_cols, tp_rows, tp_cols, P(), P(), P("ctx"), both, both,
    )
    out_specs = (both, both, both, tp_rows, tp_cols, tp_rows, tp_cols)
    return jax.shard_map(shards, mesh=mesh, in_specs=in_specs, out_specs=out_specs, check_vma=False)
```

```python
import math

import jax
import jax.numpy as jnp
from jax import lax
from jax.experimental import pallas as pl
from jax.experimental.pallas import tpu as pltpu
from jax.sharding import PartitionSpec as P

HD = 128
BETA = 0.5
NEG = -1e30
F32 = jnp.float32
BF16 = jnp.bfloat16
KB = 256


def shift(value, by):
    n = lax.axis_size("ctx")
    return lax.ppermute(value, "ctx", [(i, (i + by) % n) for i in range(n)])


def flip(value, mask):
    n = lax.axis_size("ctx")
    return lax.ppermute(value, "ctx", [(i, i ^ mask) for i in range(n)])


def spread(part):
    n_ctx, n_tp = lax.axis_size("ctx"), lax.axis_size("tp")
    per = n_ctx // n_tp
    pairs = [
        ((c + per * j) % n_ctx * n_tp + j, c * n_tp + j) for c in range(n_ctx) for j in range(n_tp)
    ]
    return lax.ppermute(part, ("ctx", "tp"), pairs)


def share_tp(rows):
    n = lax.axis_size("tp")
    return lax.all_to_all(jnp.broadcast_to(rows[None], (n,) + rows.shape), "tp", 0, 0)


def nt(left, right):
    return lax.dot_general(left, right, (((1,), (1,)), ((), ())), preferred_element_type=F32)


def nn(left, right):
    return lax.dot_general(left, right, (((1,), (0,)), ((), ())), preferred_element_type=F32)


def tn(left, right):
    return lax.dot_general(left, right, (((0,), (0,)), ((), ())), preferred_element_type=F32)


def three_parts(x):
    high = x.astype(BF16)
    rest = x - high.astype(F32)
    mid = rest.astype(BF16)
    return high, mid, (rest - mid.astype(F32)).astype(BF16)


def iota(shape, dim):
    return lax.broadcasted_iota(jnp.int32, shape, dim)


def column(row, count):
    shape = (count, row.shape[1])
    return jnp.sum(jnp.where(iota(shape, 0) == iota(shape, 1), row, 0), axis=1, keepdims=True)


def doc_bounds(len_row):
    docs = len_row.shape[1]
    shape = (docs, docs)
    end = jnp.sum(jnp.where(iota(shape, 1) <= iota(shape, 0), len_row, 0), axis=1, keepdims=True)
    return end - column(len_row, docs), end


def in_hbm(*arrays):
    return [pltpu.with_memory_space_constraint(a, pltpu.HBM) for a in arrays]


def prep_kernel(
    first_ref, len_hbm, ratio_hbm, avt_hbm, up_hbm, key_hbm, frozen_hbm, hidden_hbm, dout_hbm,
    kv_ref, rank_ref, margin_ref, start_ref, low_ref,
    len_ref, ratio_ref, avt_ref, up_ref, hidden_ref, dout_ref, sems,
):
    rows = key_hbm.shape[0]
    rank = up_ref.shape[0]
    pairs = [
        (len_hbm, len_ref), (ratio_hbm, ratio_ref), (avt_hbm, avt_ref), (up_hbm, up_ref),
        (hidden_hbm, hidden_ref), (dout_hbm, dout_ref),
        (key_hbm, kv_ref.at[0:rows]), (frozen_hbm, kv_ref.at[rows : 2 * rows]),
    ]
    copies = [pltpu.make_async_copy(src, dst, sems.at[i]) for i, (src, dst) in enumerate(pairs)]
    for copy in copies:
        copy.start()
    copies[0].wait()
    copies[1].wait()
    docs = len_ref.shape[1]
    first = first_ref[0]
    begin, end = doc_bounds(len_ref[...])
    pos = iota((1, rows), 1) + first
    own = (begin <= pos) & (pos < end)
    margin = jnp.sum(jnp.where(own, ratio_ref[...], 0.0), axis=1, keepdims=True)
    shape = (docs, 128)
    margin = jnp.sum(jnp.where(iota(shape, 0) == iota(shape, 1), margin, 0.0), axis=0, keepdims=True)
    margin = jnp.broadcast_to(margin, (8, 128))
    margin_ref[...] = jnp.zeros_like(margin_ref)
    for i, part in enumerate(three_parts(margin)):
        margin_ref[:, i * 128 : (i + 1) * 128] = part
    base = first - 3 * rows
    start = jnp.sum(jnp.where(own, begin, 0), axis=0, keepdims=True) - base
    start_ref[...] = jnp.where(iota(start_ref.shape, 0) == 0, start, pos - base)
    halves = rows // KB
    for half in range(halves):
        head = jnp.max(start[:, half * KB : half * KB + 1].astype(F32)).astype(jnp.int32)
        low_ref[half] = jnp.clip(head // KB, 0, 3 * halves + half)
    low_ref[halves] = base
    copies[2].wait()
    copies[4].wait()
    rank_ref[0:rank, :] = nt(hidden_ref[...], avt_ref[...]).T.astype(BF16)
    copies[3].wait()
    copies[5].wait()
    rank_ref[rank : 2 * rank, :] = nt(dout_ref[...], up_ref[...]).T.astype(BF16)
    copies[6].wait()
    copies[7].wait()


def prepare(first, doc_lengths, token_logratio, a_v_t, up, keys, frozen, hidden, d_out):
    rows = keys.shape[0]
    rank = up.shape[0]
    vmem = pl.BlockSpec(memory_space=pltpu.VMEM)
    return pl.pallas_call(
        prep_kernel,
        in_specs=[pl.BlockSpec(memory_space=pltpu.SMEM)] + [pl.BlockSpec(memory_space=pltpu.HBM)] * 8,
        out_specs=[vmem] * 4 + [pl.BlockSpec(memory_space=pltpu.SMEM)],
        out_shape=[
            jax.ShapeDtypeStruct((2 * rows, HD), BF16),
            jax.ShapeDtypeStruct((2 * rank, rows), BF16),
            jax.ShapeDtypeStruct((8, rows), BF16),
            jax.ShapeDtypeStruct((8, rows), jnp.int32),
            jax.ShapeDtypeStruct((rows // KB + 1,), jnp.int32),
        ],
        scratch_shapes=[
            pltpu.VMEM(a.shape, a.dtype)
            for a in (doc_lengths, token_logratio, a_v_t, up, hidden, d_out)
        ]
        + [pltpu.SemaphoreType.DMA((8,))],
        compiler_params=pltpu.CompilerParams(vmem_limit_bytes=32 * 2**20),
        name="prep",
    )(first, *in_hbm(doc_lengths, token_logratio, a_v_t, up, keys, frozen, hidden, d_out))


def margin_of(line):
    return line[:, 0:128] + line[:, 128:256] + line[:, 256:384]


def attn_kernel(
    low_ref, q_ref, g_ref, len_hbm, slot_hbm, aot_hbm, uv_hbm, start_hbm, rt_hbm, kv_far, kv_near, kv_own, far_hbm, near_hbm, own_hbm,
    o_ref, lowo_ref, z_ref, vu_ref, od_ref, weight_ref,
    len_ref, slot_ref, aot_ref, uv_ref, start_ref, rt_ref, kv, lv_far, lv_near, lv_own, sems,
    bias0, bias1, vt, r_scr, q_all, s_scr, p_scr, ot_scr, grad_all, vg,
):
    rows = q_ref.shape[0]
    heads = q_ref.shape[1] // HD
    rank = uv_ref.shape[0]
    width = 4 * rows
    n_kb = width // KB
    scale = math.log2(math.e) / math.sqrt(HD)
    halves = rows // KB

    pairs = [
        (len_hbm, len_ref), (slot_hbm, slot_ref), (aot_hbm, aot_ref), (uv_hbm, uv_ref),
        (start_hbm, start_ref), (rt_hbm, rt_ref),
        (far_hbm, lv_far), (near_hbm, lv_near), (own_hbm, lv_own),
    ]
    pairs += [(kv_far, kv.at[0:2]), (kv_near, kv.at[2]), (kv_own, kv.at[3])]
    copies = [pltpu.make_async_copy(src, dst, sems.at[i]) for i, (src, dst) in enumerate(pairs)]
    for copy in copies:
        copy.start()
    vg[...] = jnp.zeros_like(vg)
    lowo_ref[...] = jnp.zeros_like(lowo_ref)
    for copy in copies:
        copy.wait()
    biases = (bias0, bias1)
    for half in range(halves):
        start = start_ref[0:1, half * KB : (half + 1) * KB]
        qpos = start_ref[1:2, half * KB : (half + 1) * KB]
        for kb in range(n_kb):
            kpos = iota((KB, KB), 0) + kb * KB
            ok = (kpos >= start) & (kpos <= qpos)
            biases[half][kb * KB : (kb + 1) * KB, :] = jnp.where(ok, 0.0, NEG)
    r_scr[...] = rt_ref[...].astype(F32).T.astype(BF16)
    uvt = uv_ref[...].astype(F32).T.astype(BF16)
    lows = (
        lv_far[0:rank, 0:rows], lv_far[0:rank, rows : 2 * rows], lv_near[0:rank, :], lv_own[0:rank, :],
    )
    lows = [low.astype(BF16) for low in lows]
    line = lv_far[rank : rank + 1, 0:rows] + lv_far[rank : rank + 1, rows : 2 * rows]
    margin = margin_of(line + lv_near[rank : rank + 1, :] + lv_own[rank : rank + 1, :])
    docs = len_ref.shape[1]
    slots = slot_ref[...]
    slot = column(slots, docs)
    sign = (1 - 2 * (slot & 1)).astype(F32)
    sign_row = (1 - 2 * (slots & 1)).astype(F32)
    pair = jnp.where((slot >> 1) == (slots >> 1), sign_row, 0.0)
    gap = jnp.sum(pair * margin[:, 0:docs], axis=1, keepdims=True)
    weight = -BETA * sign / (1.0 + jnp.exp(BETA * gap))
    begin, end = doc_bounds(len_ref[...])
    token = iota((docs, width), 1) + low_ref[halves]
    weight = jnp.sum(jnp.where((begin <= token) & (token < end), weight, 0.0), axis=0, keepdims=True)
    weight_ref[...] = jnp.broadcast_to(weight[:, 3 * rows :], weight_ref.shape)
    for slot in range(4):
        frozen = kv[slot, rows : 2 * rows, :].astype(F32).T
        v = (frozen + 2.0 * nn(uvt, lows[slot])).astype(BF16)
        for kb in range(halves):
            vt[slot * halves + kb] = v[:, kb * KB : (kb + 1) * KB]

    for half in range(halves):
        mine = slice(half * KB, (half + 1) * KB)
        first = low_ref[half]
        last = n_kb - halves + 1 + half
        lanes = [slice(h * KB, (h + 1) * KB) for h in range(heads)]
        for h in range(heads):
            q_all[h] = q_ref[mine, h * HD : (h + 1) * HD]

        def scores(kb, peaks):
            at = pl.ds(pl.multiple_of(kb * KB, KB), KB)
            key = kv[kb // halves, pl.ds(pl.multiple_of(kb % halves * KB, KB), KB), :]
            mask = biases[half][at, :]
            new = []
            for h in range(heads):
                s = nt(key, q_all[h]) * scale + mask
                s_scr[at, lanes[h]] = s
                new.append(jnp.maximum(peaks[h], jnp.max(s.reshape(KB // 8, 8, KB), axis=0)))
            return tuple(new)

        peaks = lax.fori_loop(first, last, scores, (jnp.full((8, KB), NEG, F32),) * heads)
        tops = [jnp.max(peak, axis=0, keepdims=True) for peak in peaks]
        ot_scr[...] = jnp.zeros_like(ot_scr)

        def probs(kb, totals):
            at = pl.ds(pl.multiple_of(kb * KB, KB), KB)
            new = []
            for h in range(heads):
                e = jnp.exp2(s_scr[at, lanes[h]] - tops[h])
                new.append(totals[h] + jnp.sum(e.reshape(KB // 8, 8, KB), axis=0))
                e = e.astype(BF16)
                p_scr[at, lanes[h]] = e
                ot_scr[:, lanes[h]] += nn(vt[kb], e)
            return tuple(new)

        totals = lax.fori_loop(first, last, probs, (jnp.zeros((8, KB), F32),) * heads)
        for h in range(heads):
            cols = slice(h * HD, (h + 1) * HD)
            inv = 1.0 / jnp.sum(totals[h], axis=0, keepdims=True)
            ot = (ot_scr[:, lanes[h]] * inv).astype(BF16)
            o_ref[mine, cols] = ot.astype(F32).T.astype(BF16)
            lowo_ref[:, mine] += nn(aot_ref[:, cols], ot)
            inv_rows = jnp.broadcast_to(inv, (HD, KB)).T
            grad = g_ref[mine, cols].astype(F32) + nn(r_scr[mine, :], aot_ref[:, cols])
            grad_all[lanes[h], :] = (grad * inv_rows).astype(BF16)

        def back(kb, carry):
            at = pl.ds(pl.multiple_of(kb * KB, KB), KB)
            vg[at, :] += nn(p_scr[at, :], grad_all[...])
            return carry

        lax.fori_loop(first, last, back, 0)

    total_vg = vg[...].astype(BF16)
    z_ref[...] = nt(uv_ref[...], total_vg).astype(BF16)
    up = jnp.zeros(vu_ref.shape, F32)
    for slot in range(4):
        part = slice(slot * rows, (slot + 1) * rows)
        up += nn((weight[:, part] * lows[slot].astype(F32)).astype(BF16), total_vg[part, :])
    vu_ref[...] = (2.0 * up).astype(BF16)
    weighted_r = (weight[:, 3 * rows :] * rt_ref[...].astype(F32)).astype(BF16)
    od_ref[...] = nn(weighted_r, o_ref[...]).astype(BF16)


def attention(low, start_q, queries, cotangent, doc_lengths, pair_slots, a_o_t, r_t, kvs, lows, u_v):
    rows = queries.shape[0]
    cols = queries.shape[1]
    rank = u_v.shape[0]
    heads = cols // HD
    halves = rows // KB
    vmem = pl.BlockSpec(memory_space=pltpu.VMEM)
    anywhere = pl.BlockSpec(memory_space=pl.ANY)
    hbm = pl.BlockSpec(memory_space=pltpu.HBM)
    args = (doc_lengths, pair_slots, a_o_t, u_v)
    made = (start_q, r_t)
    scratch = [pltpu.VMEM(a.shape, a.dtype) for a in args + made]
    scratch += [pltpu.VMEM((4, 2 * rows, HD), BF16)]
    scratch += [pltpu.VMEM(a.shape, a.dtype) for a in lows]
    return pl.pallas_call(
        attn_kernel,
        in_specs=[pl.BlockSpec(memory_space=pltpu.SMEM)] + [vmem] * 2 + [hbm] * 4 + [anywhere] * 8,
        out_specs=[vmem] * 6,
        out_shape=[
            jax.ShapeDtypeStruct((rows, cols), BF16),
            jax.ShapeDtypeStruct((rank, rows), F32),
            jax.ShapeDtypeStruct((rank, 4 * rows), BF16),
            jax.ShapeDtypeStruct((rank, HD), BF16),
            jax.ShapeDtypeStruct((rank, cols), BF16),
            jax.ShapeDtypeStruct((8, rows), F32),
        ],
        scratch_shapes=scratch
        + [
            pltpu.SemaphoreType.DMA((12,)),
            pltpu.VMEM((4 * rows, KB), F32),
            pltpu.VMEM((4 * rows, KB), F32),
            pltpu.VMEM((4 * halves, HD, KB), BF16),
            pltpu.VMEM((rows, rank), BF16),
            pltpu.VMEM((heads, KB, HD), BF16),
            pltpu.VMEM((4 * rows, heads * KB), F32),
            pltpu.VMEM((4 * rows, heads * KB), BF16),
            pltpu.VMEM((HD, heads * KB), F32),
            pltpu.VMEM((heads * KB, HD), BF16),
            pltpu.VMEM((4 * rows, HD), F32),
        ],
        compiler_params=pltpu.CompilerParams(vmem_limit_bytes=48 * 2**20),
        name="attn",
    )(low, queries, cotangent, *in_hbm(*args), *made, *kvs, *lows)


def grads_kernel(shared_ref, weight_ref, vu_ref, od_ref, hidden_ref, dout_ref, sum_ref, lowo_ref, lvg_ref):
    rank = vu_ref.shape[0]
    cols = hidden_ref.shape[1]
    sums = shared_ref[0].astype(F32)
    for j in range(1, shared_ref.shape[0]):
        sums = sums + shared_ref[j].astype(F32)
    own = weight_ref[0:1, :]
    lvg = (2.0 * own * sums[0:rank]).astype(BF16)
    low_o = sums[rank : 2 * rank].astype(BF16)
    lvg_ref[...] = lvg
    lowo_ref[...] = low_o
    sum_ref[:, 0:cols] = nn(lvg, hidden_ref[...]).astype(BF16)
    sum_ref[:, cols : 2 * cols] = od_ref[...]
    weighted = (own * low_o.astype(F32)).astype(BF16)
    sum_ref[:, 2 * cols : 3 * cols] = (2.0 * nn(weighted, dout_ref[...])).astype(BF16)
    sum_ref[:, 3 * cols :] = vu_ref[...]


def grads(shared, weight, vu, od, hidden, d_out):
    rank = vu.shape[0]
    rows, cols = hidden.shape
    vmem = pl.BlockSpec(memory_space=pltpu.VMEM)
    return pl.pallas_call(
        grads_kernel,
        in_specs=[vmem] * 6,
        out_specs=[vmem] * 3,
        out_shape=[
            jax.ShapeDtypeStruct((rank, 3 * cols + HD), BF16),
            jax.ShapeDtypeStruct((rank, rows), BF16),
            jax.ShapeDtypeStruct((rank, rows), BF16),
        ],
        compiler_params=pltpu.CompilerParams(vmem_limit_bytes=32 * 2**20),
        name="grads",
    )(shared, weight, vu, od, hidden, d_out)


def shards(
    hidden, queries, rotated_keys, frozen_value_rows, adapter_a_v, value_up_matrix, adapter_a_o,
    output_up_matrix, doc_lengths, pair_slots, token_logratio, out_cotangent, attn_cotangent,
):
    rows, cols = hidden.shape
    rank = value_up_matrix.shape[0]
    first = (lax.axis_index("ctx") * rows).astype(jnp.int32)[None]
    doc_lengths = doc_lengths[None, :]
    pair_slots = pair_slots[None, :]

    kv, rank_rows, margin, start_q, low = prepare(
        first, doc_lengths, token_logratio[None, :], adapter_a_v.T, output_up_matrix, rotated_keys,
        frozen_value_rows, hidden, out_cotangent,
    )
    kv_near = shift(kv, 1)
    margin, kv_near = lax.optimization_barrier((spread(margin), kv_near))
    kv_far = shift(jnp.stack([kv_near, kv]), 2)
    sent = jnp.concatenate([rank_rows[:rank], margin, rank_rows[rank:]], axis=0)
    shared = jnp.sum(share_tp(sent).astype(F32), axis=0)
    low_own = shared[: rank + 8]
    r_t = (2.0 * shared[rank + 8 :]).astype(BF16)
    low_near = shift(low_own, 1)
    low_far = shift(jnp.concatenate([low_near, low_own], axis=1), 2)

    o, low_o_part, z, vu, od, weight = attention(
        low, start_q, queries, attn_cotangent, doc_lengths, pair_slots, adapter_a_o.T, r_t,
        (kv_far, kv_near, kv), (low_far, low_near, low_own), value_up_matrix,
    )
    z_far = shift(z[:, : 2 * rows], -2).astype(F32)
    z_near = shift((z[:, 2 * rows : 3 * rows].astype(F32) + z_far[:, :rows]).astype(BF16), -1)
    z_own = z[:, 3 * rows :].astype(F32) + z_far[:, rows:] + z_near.astype(F32)
    shared_back = share_tp(jnp.concatenate([z_own, low_o_part], axis=0).astype(BF16))

    total, low_o_t, lvg_t = grads(shared_back, weight, vu, od, hidden, out_cotangent)
    total = total.astype(F32)
    for mask in (1, 2, 4, 8, 16):
        total = lax.reduce_precision(total, 8, 7)
        total = total + flip(total.astype(BF16), mask).astype(F32)
    term = (2.0 * tn(low_o_t, output_up_matrix)).astype(BF16)
    input_grad = lax.dot_general(
        lvg_t, adapter_a_v, (((0,), (1,)), ((), ())), preferred_element_type=F32
    ).astype(BF16)
    return (
        o,
        term,
        input_grad,
        total[:, :cols].T,
        total[:, 3 * cols :],
        total[:, cols : 2 * cols].T,
        total[:, 2 * cols : 3 * cols],
    )


def solution(mesh):
    both, tp_rows, tp_cols = P("ctx", "tp"), P("tp", None), P(None, "tp")
    in_specs = (
        both, both, both, both, tp_rows, tp_cols, tp_rows, tp_cols, P(), P(), P("ctx"), both, both,
    )
    out_specs = (both, both, both, tp_rows, tp_cols, tp_rows, tp_cols)
    return jax.shard_map(shards, mesh=mesh, in_specs=in_specs, out_specs=out_specs, check_vma=False)
```

```python
import math

import jax
import jax.numpy as jnp
from jax import lax
from jax.experimental import pallas as pl
from jax.experimental.pallas import tpu as pltpu
from jax.sharding import PartitionSpec as P

HD = 128
BETA = 0.5
NEG = -1e30
F32 = jnp.float32
BF16 = jnp.bfloat16
KB = 256


def shift(value, by):
    n = lax.axis_size("ctx")
    return lax.ppermute(value, "ctx", [(i, (i + by) % n) for i in range(n)])


def flip(value, mask):
    n = lax.axis_size("ctx")
    return lax.ppermute(value, "ctx", [(i, i ^ mask) for i in range(n)])


def spread(part):
    n_ctx, n_tp = lax.axis_size("ctx"), lax.axis_size("tp")
    per = n_ctx // n_tp
    pairs = [
        ((c + per * j) % n_ctx * n_tp + j, c * n_tp + j) for c in range(n_ctx) for j in range(n_tp)
    ]
    return lax.ppermute(part, ("ctx", "tp"), pairs)


def share_tp(rows):
    n = lax.axis_size("tp")
    return lax.all_to_all(jnp.broadcast_to(rows[None], (n,) + rows.shape), "tp", 0, 0)


def nt(left, right):
    return lax.dot_general(left, right, (((1,), (1,)), ((), ())), preferred_element_type=F32)


def nn(left, right):
    return lax.dot_general(left, right, (((1,), (0,)), ((), ())), preferred_element_type=F32)


def tn(left, right):
    return lax.dot_general(left, right, (((0,), (0,)), ((), ())), preferred_element_type=F32)


def three_parts(x):
    high = x.astype(BF16)
    rest = x - high.astype(F32)
    mid = rest.astype(BF16)
    return high, mid, (rest - mid.astype(F32)).astype(BF16)


def iota(shape, dim):
    return lax.broadcasted_iota(jnp.int32, shape, dim)


def column(row, count):
    shape = (count, row.shape[1])
    return jnp.sum(jnp.where(iota(shape, 0) == iota(shape, 1), row, 0), axis=1, keepdims=True)


def doc_bounds(len_row):
    docs = len_row.shape[1]
    shape = (docs, docs)
    end = jnp.sum(jnp.where(iota(shape, 1) <= iota(shape, 0), len_row, 0), axis=1, keepdims=True)
    return end - column(len_row, docs), end


def in_hbm(*arrays):
    return [pltpu.with_memory_space_constraint(a, pltpu.HBM) for a in arrays]


def start_copies(pairs, sems):
    copies = [pltpu.make_async_copy(src, dst, sems.at[i]) for i, (src, dst) in enumerate(pairs)]
    for copy in copies:
        copy.start()
    return copies


def send_kernel(
    first_ref, len_hbm, ratio_hbm, key_hbm, frozen_hbm, kv_ref, margin_ref, len_ref, ratio_ref, sems,
):
    rows = key_hbm.shape[0]
    copies = start_copies(
        [
            (len_hbm, len_ref), (ratio_hbm, ratio_ref),
            (key_hbm, kv_ref.at[0:rows]), (frozen_hbm, kv_ref.at[rows : 2 * rows]),
        ],
        sems,
    )
    margin_ref[...] = jnp.zeros_like(margin_ref)
    copies[0].wait()
    copies[1].wait()
    docs = len_ref.shape[1]
    begin, end = doc_bounds(len_ref[...])
    pos = iota((1, rows), 1) + first_ref[0]
    own = (begin <= pos) & (pos < end)
    margin = jnp.sum(jnp.where(own, ratio_ref[...], 0.0), axis=1, keepdims=True)
    shape = (docs, 128)
    margin = jnp.sum(jnp.where(iota(shape, 0) == iota(shape, 1), margin, 0.0), axis=0, keepdims=True)
    margin = jnp.broadcast_to(margin, (8, 128))
    for i, part in enumerate(three_parts(margin)):
        margin_ref[:, i * 128 : (i + 1) * 128] = part
    copies[2].wait()
    copies[3].wait()


def to_send(first, doc_lengths, token_logratio, keys, frozen):
    rows = keys.shape[0]
    vmem = pl.BlockSpec(memory_space=pltpu.VMEM)
    return pl.pallas_call(
        send_kernel,
        in_specs=[pl.BlockSpec(memory_space=pltpu.SMEM)] + [pl.BlockSpec(memory_space=pltpu.HBM)] * 4,
        out_specs=[vmem] * 2,
        out_shape=[
            jax.ShapeDtypeStruct((2 * rows, HD), BF16),
            jax.ShapeDtypeStruct((8, rows), BF16),
        ],
        scratch_shapes=[pltpu.VMEM(a.shape, a.dtype) for a in (doc_lengths, token_logratio)]
        + [pltpu.SemaphoreType.DMA((4,))],
        name="send",
    )(first, *in_hbm(doc_lengths, token_logratio, keys, frozen))


def prep_kernel(
    first_ref, len_hbm, avt_hbm, up_hbm, hidden_hbm, dout_hbm,
    rank_ref, start_ref, low_ref,
    len_ref, avt_ref, up_ref, hidden_ref, dout_ref, sems,
):
    rows = hidden_ref.shape[0]
    rank = up_ref.shape[0]
    copies = start_copies(
        [
            (len_hbm, len_ref), (avt_hbm, avt_ref), (hidden_hbm, hidden_ref), (up_hbm, up_ref),
            (dout_hbm, dout_ref),
        ],
        sems,
    )
    copies[0].wait()
    first = first_ref[0]
    begin, end = doc_bounds(len_ref[...])
    pos = iota((1, rows), 1) + first
    own = (begin <= pos) & (pos < end)
    base = first - 3 * rows
    start = jnp.sum(jnp.where(own, begin, 0), axis=0, keepdims=True) - base
    start_ref[...] = jnp.where(iota(start_ref.shape, 0) == 0, start, pos - base)
    halves = rows // KB
    for half in range(halves):
        head = jnp.max(start[:, half * KB : half * KB + 1].astype(F32)).astype(jnp.int32)
        low_ref[half] = jnp.clip(head // KB, 0, 3 * halves + half)
    low_ref[halves] = base
    copies[1].wait()
    copies[2].wait()
    rank_ref[0:rank, :] = nt(hidden_ref[...], avt_ref[...]).T.astype(BF16)
    copies[3].wait()
    copies[4].wait()
    rank_ref[rank : 2 * rank, :] = nt(dout_ref[...], up_ref[...]).T.astype(BF16)


def prepare(first, doc_lengths, a_v_t, up, hidden, d_out):
    rows = hidden.shape[0]
    rank = up.shape[0]
    vmem = pl.BlockSpec(memory_space=pltpu.VMEM)
    smem = pl.BlockSpec(memory_space=pltpu.SMEM)
    return pl.pallas_call(
        prep_kernel,
        in_specs=[smem] + [pl.BlockSpec(memory_space=pltpu.HBM)] * 5,
        out_specs=[vmem] * 2 + [smem],
        out_shape=[
            jax.ShapeDtypeStruct((2 * rank, rows), BF16),
            jax.ShapeDtypeStruct((8, rows), jnp.int32),
            jax.ShapeDtypeStruct((rows // KB + 1,), jnp.int32),
        ],
        scratch_shapes=[pltpu.VMEM(a.shape, a.dtype) for a in (doc_lengths, a_v_t, up, hidden, d_out)]
        + [pltpu.SemaphoreType.DMA((5,))],
        compiler_params=pltpu.CompilerParams(vmem_limit_bytes=32 * 2**20),
        name="prep",
    )(first, *in_hbm(doc_lengths, a_v_t, up, hidden, d_out))


def margin_of(line):
    return line[:, 0:128] + line[:, 128:256] + line[:, 256:384]


def attn_kernel(
    low_ref, q_ref, g_ref, len_hbm, slot_hbm, aot_hbm, uv_hbm, start_hbm, rt_hbm, kv_far, kv_near, kv_own, far_hbm, near_hbm, own_hbm,
    o_ref, lowo_ref, z_ref, vu_ref, od_ref, weight_ref,
    len_ref, slot_ref, aot_ref, uv_ref, start_ref, rt_ref, kv, lv_far, lv_near, lv_own, sems,
    bias0, bias1, vt, r_scr, q_all, s_scr, p_scr, ot_scr, grad_all, vg,
):
    rows = q_ref.shape[0]
    heads = q_ref.shape[1] // HD
    rank = uv_ref.shape[0]
    width = 4 * rows
    n_kb = width // KB
    scale = math.log2(math.e) / math.sqrt(HD)
    halves = rows // KB

    pairs = [
        (len_hbm, len_ref), (slot_hbm, slot_ref), (aot_hbm, aot_ref), (uv_hbm, uv_ref),
        (start_hbm, start_ref), (rt_hbm, rt_ref),
        (far_hbm, lv_far), (near_hbm, lv_near), (own_hbm, lv_own),
    ]
    pairs += [(kv_far, kv.at[0:2]), (kv_near, kv.at[2]), (kv_own, kv.at[3])]
    copies = start_copies(pairs, sems)
    vg[...] = jnp.zeros_like(vg)
    lowo_ref[...] = jnp.zeros_like(lowo_ref)
    copies[4].wait()
    biases = (bias0, bias1)
    for half in range(halves):
        start = start_ref[0:1, half * KB : (half + 1) * KB]
        qpos = start_ref[1:2, half * KB : (half + 1) * KB]
        for kb in range(n_kb):
            kpos = iota((KB, KB), 0) + kb * KB
            ok = (kpos >= start) & (kpos <= qpos)
            biases[half][kb * KB : (kb + 1) * KB, :] = jnp.where(ok, 0.0, NEG)
    for i, copy in enumerate(copies):
        if i != 4:
            copy.wait()
    r_scr[...] = rt_ref[...].astype(F32).T.astype(BF16)
    uvt = uv_ref[...].astype(F32).T.astype(BF16)
    lows = (
        lv_far[0:rank, 0:rows], lv_far[0:rank, rows : 2 * rows], lv_near[0:rank, :], lv_own[0:rank, :],
    )
    lows = [low.astype(BF16) for low in lows]
    line = lv_far[rank : rank + 1, 0:rows] + lv_far[rank : rank + 1, rows : 2 * rows]
    margin = margin_of(line + lv_near[rank : rank + 1, :] + lv_own[rank : rank + 1, :])
    docs = len_ref.shape[1]
    slots = slot_ref[...]
    slot = column(slots, docs)
    sign = (1 - 2 * (slot & 1)).astype(F32)
    sign_row = (1 - 2 * (slots & 1)).astype(F32)
    pair = jnp.where((slot >> 1) == (slots >> 1), sign_row, 0.0)
    gap = jnp.sum(pair * margin[:, 0:docs], axis=1, keepdims=True)
    weight = -BETA * sign / (1.0 + jnp.exp(BETA * gap))
    begin, end = doc_bounds(len_ref[...])
    token = iota((docs, width), 1) + low_ref[halves]
    weight = jnp.sum(jnp.where((begin <= token) & (token < end), weight, 0.0), axis=0, keepdims=True)
    weight_ref[...] = jnp.broadcast_to(weight[:, 3 * rows :], weight_ref.shape)
    for slot in range(4):
        frozen = kv[slot, rows : 2 * rows, :].astype(F32).T
        v = (frozen + 2.0 * nn(uvt, lows[slot])).astype(BF16)
        for kb in range(halves):
            vt[slot * halves + kb] = v[:, kb * KB : (kb + 1) * KB]

    for half in range(halves):
        mine = slice(half * KB, (half + 1) * KB)
        first = low_ref[half]
        last = n_kb - halves + 1 + half
        lanes = [slice(h * KB, (h + 1) * KB) for h in range(heads)]
        for h in range(heads):
            q_all[h] = q_ref[mine, h * HD : (h + 1) * HD]

        def scores(kb, peaks):
            at = pl.ds(pl.multiple_of(kb * KB, KB), KB)
            key = kv[kb // halves, pl.ds(pl.multiple_of(kb % halves * KB, KB), KB), :]
            mask = biases[half][at, :]
            new = []
            for h in range(heads):
                s = nt(key, q_all[h]) * scale + mask
                s_scr[at, lanes[h]] = s
                new.append(jnp.maximum(peaks[h], jnp.max(s.reshape(KB // 8, 8, KB), axis=0)))
            return tuple(new)

        peaks = lax.fori_loop(first, last, scores, (jnp.full((8, KB), NEG, F32),) * heads)
        tops = [jnp.max(peak, axis=0, keepdims=True) for peak in peaks]
        ot_scr[...] = jnp.zeros_like(ot_scr)

        def probs(kb, totals):
            at = pl.ds(pl.multiple_of(kb * KB, KB), KB)
            new = []
            for h in range(heads):
                e = jnp.exp2(s_scr[at, lanes[h]] - tops[h])
                new.append(totals[h] + jnp.sum(e.reshape(KB // 8, 8, KB), axis=0))
                e = e.astype(BF16)
                p_scr[at, lanes[h]] = e
                ot_scr[:, lanes[h]] += nn(vt[kb], e)
            return tuple(new)

        totals = lax.fori_loop(first, last, probs, (jnp.zeros((8, KB), F32),) * heads)
        for h in range(heads):
            cols = slice(h * HD, (h + 1) * HD)
            inv = 1.0 / jnp.sum(totals[h], axis=0, keepdims=True)
            ot = (ot_scr[:, lanes[h]] * inv).astype(BF16)
            o_ref[mine, cols] = ot.astype(F32).T.astype(BF16)
            lowo_ref[:, mine] += nn(aot_ref[:, cols], ot)
            inv_rows = jnp.broadcast_to(inv, (HD, KB)).T
            grad = g_ref[mine, cols].astype(F32) + nn(r_scr[mine, :], aot_ref[:, cols])
            grad_all[lanes[h], :] = (grad * inv_rows).astype(BF16)

        def back(kb, carry):
            at = pl.ds(pl.multiple_of(kb * KB, KB), KB)
            vg[at, :] += nn(p_scr[at, :], grad_all[...])
            return carry

        lax.fori_loop(first, last, back, 0)

    total_vg = vg[...].astype(BF16)
    z_ref[...] = nt(uv_ref[...], total_vg).astype(BF16)
    up = jnp.zeros(vu_ref.shape, F32)
    for slot in range(4):
        part = slice(slot * rows, (slot + 1) * rows)
        up += nn((weight[:, part] * lows[slot].astype(F32)).astype(BF16), total_vg[part, :])
    vu_ref[...] = (2.0 * up).astype(BF16)
    weighted_r = (weight[:, 3 * rows :] * rt_ref[...].astype(F32)).astype(BF16)
    od_ref[...] = nn(weighted_r, o_ref[...]).astype(BF16)


def attention(low, start_q, queries, cotangent, doc_lengths, pair_slots, a_o_t, r_t, kvs, lows, u_v):
    rows = queries.shape[0]
    cols = queries.shape[1]
    rank = u_v.shape[0]
    heads = cols // HD
    halves = rows // KB
    vmem = pl.BlockSpec(memory_space=pltpu.VMEM)
    anywhere = pl.BlockSpec(memory_space=pl.ANY)
    hbm = pl.BlockSpec(memory_space=pltpu.HBM)
    args = (doc_lengths, pair_slots, a_o_t, u_v)
    made = (start_q, r_t)
    scratch = [pltpu.VMEM(a.shape, a.dtype) for a in args + made]
    scratch += [pltpu.VMEM((4, 2 * rows, HD), BF16)]
    scratch += [pltpu.VMEM(a.shape, a.dtype) for a in lows]
    return pl.pallas_call(
        attn_kernel,
        in_specs=[pl.BlockSpec(memory_space=pltpu.SMEM)] + [vmem] * 2 + [hbm] * 4 + [anywhere] * 8,
        out_specs=[vmem] * 6,
        out_shape=[
            jax.ShapeDtypeStruct((rows, cols), BF16),
            jax.ShapeDtypeStruct((rank, rows), F32),
            jax.ShapeDtypeStruct((rank, 4 * rows), BF16),
            jax.ShapeDtypeStruct((rank, HD), BF16),
            jax.ShapeDtypeStruct((rank, cols), BF16),
            jax.ShapeDtypeStruct((8, rows), F32),
        ],
        scratch_shapes=scratch
        + [
            pltpu.SemaphoreType.DMA((12,)),
            pltpu.VMEM((4 * rows, KB), F32),
            pltpu.VMEM((4 * rows, KB), F32),
            pltpu.VMEM((4 * halves, HD, KB), BF16),
            pltpu.VMEM((rows, rank), BF16),
            pltpu.VMEM((heads, KB, HD), BF16),
            pltpu.VMEM((4 * rows, heads * KB), F32),
            pltpu.VMEM((4 * rows, heads * KB), BF16),
            pltpu.VMEM((HD, heads * KB), F32),
            pltpu.VMEM((heads * KB, HD), BF16),
            pltpu.VMEM((4 * rows, HD), F32),
        ],
        compiler_params=pltpu.CompilerParams(vmem_limit_bytes=48 * 2**20),
        name="attn",
    )(low, queries, cotangent, *in_hbm(*args), *made, *kvs, *lows)


def grads_kernel(shared_ref, weight_ref, vu_ref, od_ref, hidden_ref, dout_ref, sum_ref, lowo_ref, lvg_ref):
    rank = vu_ref.shape[0]
    cols = hidden_ref.shape[1]
    sums = shared_ref[0].astype(F32)
    for j in range(1, shared_ref.shape[0]):
        sums = sums + shared_ref[j].astype(F32)
    own = weight_ref[0:1, :]
    lvg = (2.0 * own * sums[0:rank]).astype(BF16)
    low_o = sums[rank : 2 * rank].astype(BF16)
    lvg_ref[...] = lvg
    lowo_ref[...] = low_o
    sum_ref[:, 0:cols] = nn(lvg, hidden_ref[...]).astype(BF16)
    sum_ref[:, cols : 2 * cols] = od_ref[...]
    weighted = (own * low_o.astype(F32)).astype(BF16)
    sum_ref[:, 2 * cols : 3 * cols] = (2.0 * nn(weighted, dout_ref[...])).astype(BF16)
    sum_ref[:, 3 * cols :] = vu_ref[...]


def grads(shared, weight, vu, od, hidden, d_out):
    rank = vu.shape[0]
    rows, cols = hidden.shape
    vmem = pl.BlockSpec(memory_space=pltpu.VMEM)
    return pl.pallas_call(
        grads_kernel,
        in_specs=[vmem] * 6,
        out_specs=[vmem] * 3,
        out_shape=[
            jax.ShapeDtypeStruct((rank, 3 * cols + HD), BF16),
            jax.ShapeDtypeStruct((rank, rows), BF16),
            jax.ShapeDtypeStruct((rank, rows), BF16),
        ],
        compiler_params=pltpu.CompilerParams(vmem_limit_bytes=32 * 2**20),
        name="grads",
    )(shared, weight, vu, od, hidden, d_out)


def shards(
    hidden, queries, rotated_keys, frozen_value_rows, adapter_a_v, value_up_matrix, adapter_a_o,
    output_up_matrix, doc_lengths, pair_slots, token_logratio, out_cotangent, attn_cotangent,
):
    rows, cols = hidden.shape
    rank = value_up_matrix.shape[0]
    first = (lax.axis_index("ctx") * rows).astype(jnp.int32)[None]
    doc_lengths = doc_lengths[None, :]
    pair_slots = pair_slots[None, :]

    kv, margin = to_send(first, doc_lengths, token_logratio[None, :], rotated_keys, frozen_value_rows)
    rank_rows, start_q, low = prepare(
        first, doc_lengths, adapter_a_v.T, output_up_matrix, hidden, out_cotangent
    )
    kv_near = shift(kv, 1)
    margin, kv_near = lax.optimization_barrier((spread(margin), kv_near))
    kv_far = shift(jnp.stack([kv_near, kv]), 2)
    sent = jnp.concatenate([rank_rows[:rank], margin, rank_rows[rank:]], axis=0)
    shared = jnp.sum(share_tp(sent).astype(F32), axis=0)
    low_own = shared[: rank + 8]
    r_t = (2.0 * shared[rank + 8 :]).astype(BF16)
    low_near = shift(low_own, 1)
    low_far = shift(jnp.concatenate([low_near, low_own], axis=1), 2)

    o, low_o_part, z, vu, od, weight = attention(
        low, start_q, queries, attn_cotangent, doc_lengths, pair_slots, adapter_a_o.T, r_t,
        (kv_far, kv_near, kv), (low_far, low_near, low_own), value_up_matrix,
    )
    z_far = shift(z[:, : 2 * rows], -2).astype(F32)
    z_near = shift((z[:, 2 * rows : 3 * rows].astype(F32) + z_far[:, :rows]).astype(BF16), -1)
    z_own = z[:, 3 * rows :].astype(F32) + z_far[:, rows:] + z_near.astype(F32)
    shared_back = share_tp(jnp.concatenate([z_own, low_o_part], axis=0).astype(BF16))

    total, low_o_t, lvg_t = grads(shared_back, weight, vu, od, hidden, out_cotangent)
    total = total.astype(F32)
    for mask in (1, 2, 4, 8, 16):
        total = lax.reduce_precision(total, 8, 7)
        total = total + flip(total.astype(BF16), mask).astype(F32)
    term = (2.0 * tn(low_o_t, output_up_matrix)).astype(BF16)
    input_grad = lax.dot_general(
        lvg_t, adapter_a_v, (((0,), (1,)), ((), ())), preferred_element_type=F32
    ).astype(BF16)
    return (
        o,
        term,
        input_grad,
        total[:, :cols].T,
        total[:, 3 * cols :],
        total[:, cols : 2 * cols].T,
        total[:, 2 * cols : 3 * cols],
    )


def solution(mesh):
    both, tp_rows, tp_cols = P("ctx", "tp"), P("tp", None), P(None, "tp")
    in_specs = (
        both, both, both, both, tp_rows, tp_cols, tp_rows, tp_cols, P(), P(), P("ctx"), both, both,
    )
    out_specs = (both, both, both, tp_rows, tp_cols, tp_rows, tp_cols)
    return jax.shard_map(shards, mesh=mesh, in_specs=in_specs, out_specs=out_specs, check_vma=False)
```

```python
import math

import jax
import jax.numpy as jnp
from jax import lax
from jax.experimental import pallas as pl
from jax.experimental.pallas import tpu as pltpu
from jax.sharding import PartitionSpec as P

HD = 128
BETA = 0.5
NEG = -1e30
F32 = jnp.float32
BF16 = jnp.bfloat16
KB = 256


def shift(value, by):
    n = lax.axis_size("ctx")
    return lax.ppermute(value, "ctx", [(i, (i + by) % n) for i in range(n)])


def flip(value, mask):
    n = lax.axis_size("ctx")
    return lax.ppermute(value, "ctx", [(i, i ^ mask) for i in range(n)])


def spread(part):
    n_ctx, n_tp = lax.axis_size("ctx"), lax.axis_size("tp")
    per = n_ctx // n_tp
    pairs = [
        ((c + per * j) % n_ctx * n_tp + j, c * n_tp + j) for c in range(n_ctx) for j in range(n_tp)
    ]
    return lax.ppermute(part, ("ctx", "tp"), pairs)


def share_tp(rows):
    n = lax.axis_size("tp")
    return lax.all_to_all(jnp.broadcast_to(rows[None], (n,) + rows.shape), "tp", 0, 0)


def nt(left, right):
    return lax.dot_general(left, right, (((1,), (1,)), ((), ())), preferred_element_type=F32)


def nn(left, right):
    return lax.dot_general(left, right, (((1,), (0,)), ((), ())), preferred_element_type=F32)


def tn(left, right):
    return lax.dot_general(left, right, (((0,), (0,)), ((), ())), preferred_element_type=F32)


def three_parts(x):
    high = x.astype(BF16)
    rest = x - high.astype(F32)
    mid = rest.astype(BF16)
    return high, mid, (rest - mid.astype(F32)).astype(BF16)


def iota(shape, dim):
    return lax.broadcasted_iota(jnp.int32, shape, dim)


def column(row, count):
    shape = (count, row.shape[1])
    return jnp.sum(jnp.where(iota(shape, 0) == iota(shape, 1), row, 0), axis=1, keepdims=True)


def doc_bounds(len_row):
    docs = len_row.shape[1]
    shape = (docs, docs)
    end = jnp.sum(jnp.where(iota(shape, 1) <= iota(shape, 0), len_row, 0), axis=1, keepdims=True)
    return end - column(len_row, docs), end


def in_hbm(*arrays):
    return [pltpu.with_memory_space_constraint(a, pltpu.HBM) for a in arrays]


def start_copies(pairs, sems):
    copies = [pltpu.make_async_copy(src, dst, sems.at[i]) for i, (src, dst) in enumerate(pairs)]
    for copy in copies:
        copy.start()
    return copies


def send_kernel(
    first_ref, len_hbm, ratio_hbm, key_hbm, frozen_hbm, kv_ref, margin_ref, len_ref, ratio_ref, sems,
):
    rows = key_hbm.shape[0]
    copies = start_copies(
        [
            (len_hbm, len_ref), (ratio_hbm, ratio_ref),
            (key_hbm, kv_ref.at[0:rows]), (frozen_hbm, kv_ref.at[rows : 2 * rows]),
        ],
        sems,
    )
    margin_ref[...] = jnp.zeros_like(margin_ref)
    copies[0].wait()
    copies[1].wait()
    docs = len_ref.shape[1]
    begin, end = doc_bounds(len_ref[...])
    pos = iota((1, rows), 1) + first_ref[0]
    own = (begin <= pos) & (pos < end)
    margin = jnp.sum(jnp.where(own, ratio_ref[...], 0.0), axis=1, keepdims=True)
    shape = (docs, 128)
    margin = jnp.sum(jnp.where(iota(shape, 0) == iota(shape, 1), margin, 0.0), axis=0, keepdims=True)
    margin = jnp.broadcast_to(margin, (8, 128))
    for i, part in enumerate(three_parts(margin)):
        margin_ref[:, i * 128 : (i + 1) * 128] = part
    copies[2].wait()
    copies[3].wait()


def to_send(first, doc_lengths, token_logratio, keys, frozen):
    rows = keys.shape[0]
    vmem = pl.BlockSpec(memory_space=pltpu.VMEM)
    return pl.pallas_call(
        send_kernel,
        in_specs=[pl.BlockSpec(memory_space=pltpu.SMEM)] + [pl.BlockSpec(memory_space=pltpu.HBM)] * 4,
        out_specs=[vmem] * 2,
        out_shape=[
            jax.ShapeDtypeStruct((2 * rows, HD), BF16),
            jax.ShapeDtypeStruct((8, rows), BF16),
        ],
        scratch_shapes=[pltpu.VMEM(a.shape, a.dtype) for a in (doc_lengths, token_logratio)]
        + [pltpu.SemaphoreType.DMA((4,))],
        name="send",
    )(first, *in_hbm(doc_lengths, token_logratio, keys, frozen))


def prep_kernel(
    first_ref, len_hbm, avt_hbm, up_hbm, hidden_hbm, dout_hbm,
    rank_ref, start_ref, low_ref,
    len_ref, avt_ref, up_ref, hidden_ref, dout_ref, sems,
):
    rows = hidden_ref.shape[0]
    rank = up_ref.shape[0]
    copies = start_copies(
        [
            (len_hbm, len_ref), (avt_hbm, avt_ref), (hidden_hbm, hidden_ref), (up_hbm, up_ref),
            (dout_hbm, dout_ref),
        ],
        sems,
    )
    copies[0].wait()
    first = first_ref[0]
    begin, end = doc_bounds(len_ref[...])
    pos = iota((1, rows), 1) + first
    own = (begin <= pos) & (pos < end)
    base = first - 3 * rows
    start = jnp.sum(jnp.where(own, begin, 0), axis=0, keepdims=True) - base
    start_ref[...] = jnp.where(iota(start_ref.shape, 0) == 0, start, pos - base)
    halves = rows // KB
    for half in range(halves):
        head = jnp.max(start[:, half * KB : half * KB + 1].astype(F32)).astype(jnp.int32)
        low_ref[half] = jnp.clip(head // KB, 0, 3 * halves + half)
    low_ref[halves] = base
    copies[1].wait()
    copies[2].wait()
    rank_ref[0:rank, :] = nt(hidden_ref[...], avt_ref[...]).T.astype(BF16)
    copies[3].wait()
    copies[4].wait()
    rank_ref[rank : 2 * rank, :] = nt(dout_ref[...], up_ref[...]).T.astype(BF16)


def prepare(first, doc_lengths, a_v_t, up, hidden, d_out):
    rows = hidden.shape[0]
    rank = up.shape[0]
    vmem = pl.BlockSpec(memory_space=pltpu.VMEM)
    smem = pl.BlockSpec(memory_space=pltpu.SMEM)
    return pl.pallas_call(
        prep_kernel,
        in_specs=[smem] + [pl.BlockSpec(memory_space=pltpu.HBM)] * 5,
        out_specs=[vmem] * 2 + [smem],
        out_shape=[
            jax.ShapeDtypeStruct((2 * rank, rows), BF16),
            jax.ShapeDtypeStruct((8, rows), jnp.int32),
            jax.ShapeDtypeStruct((rows // KB + 1,), jnp.int32),
        ],
        scratch_shapes=[pltpu.VMEM(a.shape, a.dtype) for a in (doc_lengths, a_v_t, up, hidden, d_out)]
        + [pltpu.SemaphoreType.DMA((5,))],
        compiler_params=pltpu.CompilerParams(vmem_limit_bytes=32 * 2**20),
        name="prep",
    )(first, *in_hbm(doc_lengths, a_v_t, up, hidden, d_out))


def margin_of(line):
    return line[:, 0:128] + line[:, 128:256] + line[:, 256:384]


def attn_kernel(
    low_ref, q_ref, g_ref, len_hbm, slot_hbm, aot_hbm, uv_hbm, start_hbm, rt_hbm, kv_far, kv_near, kv_own, far_hbm, near_hbm, own_hbm,
    o_ref, lowo_ref, z_ref, vu_ref, od_ref, weight_ref,
    len_ref, slot_ref, aot_ref, uv_ref, start_ref, rt_ref, kv, lv_far, lv_near, lv_own, sems,
    bias0, bias1, vt, r_scr, q_all, s_scr, p_scr, ot_scr, grad_all, vg,
):
    rows = q_ref.shape[0]
    heads = q_ref.shape[1] // HD
    rank = uv_ref.shape[0]
    width = 4 * rows
    n_kb = width // KB
    scale = math.log2(math.e) / math.sqrt(HD)
    halves = rows // KB

    pairs = [
        (len_hbm, len_ref), (slot_hbm, slot_ref), (aot_hbm, aot_ref), (uv_hbm, uv_ref),
        (start_hbm, start_ref), (rt_hbm, rt_ref),
        (far_hbm, lv_far), (near_hbm, lv_near), (own_hbm, lv_own),
    ]
    pairs += [(kv_far, kv.at[0:2]), (kv_near, kv.at[2]), (kv_own, kv.at[3])]
    copies = start_copies(pairs, sems)
    vg[...] = jnp.zeros_like(vg)
    lowo_ref[...] = jnp.zeros_like(lowo_ref)
    copies[4].wait()
    biases = (bias0, bias1)
    for half in range(halves):
        start = start_ref[0:1, half * KB : (half + 1) * KB]
        qpos = start_ref[1:2, half * KB : (half + 1) * KB]
        for kb in range(n_kb):
            kpos = iota((KB, KB), 0) + kb * KB
            ok = (kpos >= start) & (kpos <= qpos)
            biases[half][kb * KB : (kb + 1) * KB, :] = jnp.where(ok, 0.0, NEG)
    for i, copy in enumerate(copies):
        if i != 4:
            copy.wait()
    r_scr[...] = rt_ref[...].astype(F32).T.astype(BF16)
    uvt = uv_ref[...].astype(F32).T.astype(BF16)
    lows = (
        lv_far[0:rank, 0:rows], lv_far[0:rank, rows : 2 * rows], lv_near[0:rank, :], lv_own[0:rank, :],
    )
    lows = [low.astype(BF16) for low in lows]
    line = lv_far[rank : rank + 1, 0:rows] + lv_far[rank : rank + 1, rows : 2 * rows]
    margin = margin_of(line + lv_near[rank : rank + 1, :] + lv_own[rank : rank + 1, :])
    docs = len_ref.shape[1]
    slots = slot_ref[...]
    slot = column(slots, docs)
    sign = (1 - 2 * (slot & 1)).astype(F32)
    sign_row = (1 - 2 * (slots & 1)).astype(F32)
    pair = jnp.where((slot >> 1) == (slots >> 1), sign_row, 0.0)
    gap = jnp.sum(pair * margin[:, 0:docs], axis=1, keepdims=True)
    weight = -BETA * sign / (1.0 + jnp.exp(BETA * gap))
    begin, end = doc_bounds(len_ref[...])
    token = iota((docs, width), 1) + low_ref[halves]
    weight = jnp.sum(jnp.where((begin <= token) & (token < end), weight, 0.0), axis=0, keepdims=True)
    weight_ref[...] = jnp.broadcast_to(weight[:, 3 * rows :], weight_ref.shape)
    for slot in range(4):
        frozen = kv[slot, rows : 2 * rows, :].astype(F32).T
        v = (frozen + 2.0 * nn(uvt, lows[slot])).astype(BF16)
        for kb in range(halves):
            vt[slot * halves + kb] = v[:, kb * KB : (kb + 1) * KB]

    for half in range(halves):
        mine = slice(half * KB, (half + 1) * KB)
        first = low_ref[half]
        last = n_kb - halves + 1 + half
        lanes = [slice(h * KB, (h + 1) * KB) for h in range(heads)]
        for h in range(heads):
            q_all[h] = q_ref[mine, h * HD : (h + 1) * HD]

        def scores(kb, peaks):
            at = pl.ds(pl.multiple_of(kb * KB, KB), KB)
            key = kv[kb // halves, pl.ds(pl.multiple_of(kb % halves * KB, KB), KB), :]
            mask = biases[half][at, :]
            new = []
            for h in range(heads):
                s = nt(key, q_all[h]) * scale + mask
                s_scr[at, lanes[h]] = s
                new.append(jnp.maximum(peaks[h], jnp.max(s.reshape(KB // 8, 8, KB), axis=0)))
            return tuple(new)

        peaks = lax.fori_loop(first, last, scores, (jnp.full((8, KB), NEG, F32),) * heads)
        tops = [jnp.max(peak, axis=0, keepdims=True) for peak in peaks]
        ot_scr[...] = jnp.zeros_like(ot_scr)

        def probs(kb, totals):
            at = pl.ds(pl.multiple_of(kb * KB, KB), KB)
            new = []
            for h in range(heads):
                e = jnp.exp2(s_scr[at, lanes[h]] - tops[h])
                new.append(totals[h] + jnp.sum(e.reshape(KB // 8, 8, KB), axis=0))
                e = e.astype(BF16)
                p_scr[at, lanes[h]] = e
                ot_scr[:, lanes[h]] += nn(vt[kb], e)
            return tuple(new)

        totals = lax.fori_loop(first, last, probs, (jnp.zeros((8, KB), F32),) * heads)
        for h in range(heads):
            cols = slice(h * HD, (h + 1) * HD)
            inv = 1.0 / jnp.sum(totals[h], axis=0, keepdims=True)
            ot = (ot_scr[:, lanes[h]] * inv).astype(BF16)
            o_ref[mine, cols] = ot.astype(F32).T.astype(BF16)
            lowo_ref[:, mine] += nn(aot_ref[:, cols], ot)
            inv_rows = jnp.broadcast_to(inv, (HD, KB)).T
            grad = g_ref[mine, cols].astype(F32) + nn(r_scr[mine, :], aot_ref[:, cols])
            grad_all[lanes[h], :] = (grad * inv_rows).astype(BF16)

        def back(kb, carry):
            at = pl.ds(pl.multiple_of(kb * KB, KB), KB)
            vg[at, :] += nn(p_scr[at, :], grad_all[...])
            return carry

        lax.fori_loop(first, last, back, 0)

    total_vg = vg[...].astype(BF16)
    z_ref[...] = nt(uv_ref[...], total_vg).astype(BF16)
    up = jnp.zeros(vu_ref.shape, F32)
    for slot in range(4):
        part = slice(slot * rows, (slot + 1) * rows)
        up += nn((weight[:, part] * lows[slot].astype(F32)).astype(BF16), total_vg[part, :])
    vu_ref[...] = (2.0 * up).astype(BF16)
    weighted_r = (weight[:, 3 * rows :] * rt_ref[...].astype(F32)).astype(BF16)
    od_ref[...] = nn(weighted_r, o_ref[...]).astype(BF16)


def attention(low, start_q, queries, cotangent, doc_lengths, pair_slots, a_o_t, r_t, kvs, lows, u_v):
    rows = queries.shape[0]
    cols = queries.shape[1]
    rank = u_v.shape[0]
    heads = cols // HD
    halves = rows // KB
    vmem = pl.BlockSpec(memory_space=pltpu.VMEM)
    anywhere = pl.BlockSpec(memory_space=pl.ANY)
    hbm = pl.BlockSpec(memory_space=pltpu.HBM)
    args = (doc_lengths, pair_slots, a_o_t, u_v)
    made = (start_q, r_t)
    scratch = [pltpu.VMEM(a.shape, a.dtype) for a in args + made]
    scratch += [pltpu.VMEM((4, 2 * rows, HD), BF16)]
    scratch += [pltpu.VMEM(a.shape, a.dtype) for a in lows]
    return pl.pallas_call(
        attn_kernel,
        in_specs=[pl.BlockSpec(memory_space=pltpu.SMEM)] + [vmem] * 2 + [hbm] * 4 + [anywhere] * 8,
        out_specs=[vmem] * 6,
        out_shape=[
            jax.ShapeDtypeStruct((rows, cols), BF16),
            jax.ShapeDtypeStruct((rank, rows), F32),
            jax.ShapeDtypeStruct((rank, 4 * rows), BF16),
            jax.ShapeDtypeStruct((rank, HD), BF16),
            jax.ShapeDtypeStruct((rank, cols), BF16),
            jax.ShapeDtypeStruct((8, rows), F32),
        ],
        scratch_shapes=scratch
        + [
            pltpu.SemaphoreType.DMA((12,)),
            pltpu.VMEM((4 * rows, KB), F32),
            pltpu.VMEM((4 * rows, KB), F32),
            pltpu.VMEM((4 * halves, HD, KB), BF16),
            pltpu.VMEM((rows, rank), BF16),
            pltpu.VMEM((heads, KB, HD), BF16),
            pltpu.VMEM((4 * rows, heads * KB), F32),
            pltpu.VMEM((4 * rows, heads * KB), BF16),
            pltpu.VMEM((HD, heads * KB), F32),
            pltpu.VMEM((heads * KB, HD), BF16),
            pltpu.VMEM((4 * rows, HD), F32),
        ],
        compiler_params=pltpu.CompilerParams(vmem_limit_bytes=48 * 2**20),
        name="attn",
    )(low, queries, cotangent, *in_hbm(*args), *made, *kvs, *lows)


def grads_kernel(
    side_ref, shared_ref, weight_ref, vu_ref, od_ref, hidden_ref, dout_ref, kept_ref, sent_ref, lowo_ref, lvg_ref
):
    rank = vu_ref.shape[0]
    half = kept_ref.shape[1]
    sums = shared_ref[0].astype(F32)
    for j in range(1, shared_ref.shape[0]):
        sums = sums + shared_ref[j].astype(F32)
    own = weight_ref[0:1, :]
    lvg = (2.0 * own * sums[0:rank]).astype(BF16)
    low_o = sums[rank : 2 * rank].astype(BF16)
    lvg_ref[...] = lvg
    lowo_ref[...] = low_o
    vd = nn(lvg, hidden_ref[...])
    weighted = (own * low_o.astype(F32)).astype(BF16)
    ou = 2.0 * nn(weighted, dout_ref[...])
    parts = [vd, od_ref[...].astype(F32), ou, vu_ref[...].astype(F32)]
    whole = jnp.concatenate(parts + [jnp.zeros((rank, 128), F32)], axis=1)
    left = side_ref[0] == 0
    kept_ref[...] = jnp.where(left, whole[:, :half], whole[:, half:]).astype(BF16)
    sent_ref[...] = jnp.where(left, whole[:, half:], whole[:, :half]).astype(BF16)


def grads(side, shared, weight, vu, od, hidden, d_out):
    rank = vu.shape[0]
    rows, cols = hidden.shape
    half = (3 * cols + HD + 128) // 2
    vmem = pl.BlockSpec(memory_space=pltpu.VMEM)
    return pl.pallas_call(
        grads_kernel,
        in_specs=[pl.BlockSpec(memory_space=pltpu.SMEM)] + [vmem] * 6,
        out_specs=[vmem] * 4,
        out_shape=[
            jax.ShapeDtypeStruct((rank, half), BF16),
            jax.ShapeDtypeStruct((rank, half), BF16),
            jax.ShapeDtypeStruct((rank, rows), BF16),
            jax.ShapeDtypeStruct((rank, rows), BF16),
        ],
        compiler_params=pltpu.CompilerParams(vmem_limit_bytes=32 * 2**20),
        name="grads",
    )(side, shared, weight, vu, od, hidden, d_out)


def shards(
    hidden, queries, rotated_keys, frozen_value_rows, adapter_a_v, value_up_matrix, adapter_a_o,
    output_up_matrix, doc_lengths, pair_slots, token_logratio, out_cotangent, attn_cotangent,
):
    rows, cols = hidden.shape
    rank = value_up_matrix.shape[0]
    first = (lax.axis_index("ctx") * rows).astype(jnp.int32)[None]
    doc_lengths = doc_lengths[None, :]
    pair_slots = pair_slots[None, :]

    kv, margin = to_send(first, doc_lengths, token_logratio[None, :], rotated_keys, frozen_value_rows)
    rank_rows, start_q, low = prepare(
        first, doc_lengths, adapter_a_v.T, output_up_matrix, hidden, out_cotangent
    )
    kv_near = shift(kv, 1)
    margin, kv_near = lax.optimization_barrier((spread(margin), kv_near))
    kv_far = shift(jnp.stack([kv_near, kv]), 2)
    sent = jnp.concatenate([rank_rows[:rank], margin, rank_rows[rank:]], axis=0)
    shared = jnp.sum(share_tp(sent).astype(F32), axis=0)
    low_own = shared[: rank + 8]
    r_t = (2.0 * shared[rank + 8 :]).astype(BF16)
    low_near = shift(low_own, 1)
    low_far = shift(jnp.concatenate([low_near, low_own], axis=1), 2)

    o, low_o_part, z, vu, od, weight = attention(
        low, start_q, queries, attn_cotangent, doc_lengths, pair_slots, adapter_a_o.T, r_t,
        (kv_far, kv_near, kv), (low_far, low_near, low_own), value_up_matrix,
    )
    z_far = shift(z[:, : 2 * rows], -2).astype(F32)
    z_near = shift((z[:, 2 * rows : 3 * rows].astype(F32) + z_far[:, :rows]).astype(BF16), -1)
    z_own = z[:, 3 * rows :].astype(F32) + z_far[:, rows:] + z_near.astype(F32)
    shared_back = share_tp(jnp.concatenate([z_own, low_o_part], axis=0).astype(BF16))

    side = (lax.axis_index("ctx") % 2).astype(jnp.int32)
    kept, given, low_o_t, lvg_t = grads(side[None], shared_back, weight, vu, od, hidden, out_cotangent)
    total = kept.astype(F32) + flip(given, 1).astype(F32)
    for mask in (2, 4, 8, 16):
        total = lax.reduce_precision(total, 8, 7)
        total = total + flip(total.astype(BF16), mask).astype(F32)
    total = lax.reduce_precision(total, 8, 7)
    other = flip(total.astype(BF16), 1).astype(F32)
    left = side == 0
    total = jnp.concatenate([jnp.where(left, total, other), jnp.where(left, other, total)], axis=1)
    term = (2.0 * tn(low_o_t, output_up_matrix)).astype(BF16)
    input_grad = lax.dot_general(
        lvg_t, adapter_a_v, (((0,), (1,)), ((), ())), preferred_element_type=F32
    ).astype(BF16)
    return (
        o,
        term,
        input_grad,
        total[:, :cols].T,
        total[:, 3 * cols : 3 * cols + HD],
        total[:, cols : 2 * cols].T,
        total[:, 2 * cols : 3 * cols],
    )


def solution(mesh):
    both, tp_rows, tp_cols = P("ctx", "tp"), P("tp", None), P(None, "tp")
    in_specs = (
        both, both, both, both, tp_rows, tp_cols, tp_rows, tp_cols, P(), P(), P("ctx"), both, both,
    )
    out_specs = (both, both, both, tp_rows, tp_cols, tp_rows, tp_cols)
    return jax.shard_map(shards, mesh=mesh, in_specs=in_specs, out_specs=out_specs, check_vma=False)
```
